32 devices in a mesh: band: 2 (over y), gx: 8 (over z, x), gy: 2 (over core).
Axes of the slice: x: 2, y: 2, z: 4, core: 2. Of those that a mesh axis runs over, the one named last changes fastest.
Arguments:
- series: float32 [32768, 256], P(('band', 'gx', 'gy')), parts along dimension 0, may hold values from -6 to 6
- templates: bfloat16 [16, 2, 128], replicated, may hold values from -0.125 to 0.125
- drift: int32 [16], replicated, may hold values from 0 to 127, as said below
Outputs:
- band_power: float32 [32768, 128], P(('band', 'gx', 'gy')), parts along dimension 0
The draws below stay inside these ranges and needn't reach their ends.
There are 2 independent parts, one for each index of `band`. The reference program is written for one: setup_inputs(seed, part) draws one part's arguments, and reference() takes and returns one part's arrays. A program takes and returns all parts, laid end to end along the dimension named above; an argument that names none is the same for every part. Nothing has to cross between parts.
Inputs may be any that keep to these rules, and one draw needn't show every extreme that they name: `drift`: some template has shift 0 and some has shift 128 - 1.
All inputs are finite; a program needn't handle non-finite values.
Results may differ from the reference program's by a relative error of at most 0.0011.
Values may be sent and summed in bfloat16 or wider, within the bound.
No kernel may reach another device: no remote copies, remote signals or barrier semaphores. Data moves between devices by JAX's collectives and lax.ppermute only.
A program may use at most 192 MiB of HBM per device.

```python
import math
import jax
import jax.numpy as jnp
from jax import lax

TEMPLATES = 16
TAPS = 128
LENGTH = 4194304
BINS = 2097152


def draw_drift(key, part):
    shift_key, rank_key = jax.random.split(key)
    values = jax.random.randint(shift_key, (TEMPLATES,), 0, TAPS, dtype=jnp.int32)
    ranking = jax.random.permutation(rank_key, TEMPLATES)
    positions = jnp.arange(TEMPLATES, dtype=jnp.int32)
    values = jnp.where(positions == ranking[0], TAPS - 1, values)
    values = jnp.where(positions == ranking[1], 0, values)
    return values.astype(jnp.int32)


def levels(stream_key, shape, shards, low, largest):
    level, own = 1.0, jax.random.fold_in(stream_key, 6)
    for position, blocks in shards:
        heights = jnp.exp(jax.random.uniform(jax.random.fold_in(own, position), (blocks,), jnp.float32, low / len(shards), largest / len(shards)))
        level = level * jnp.repeat(heights, shape[position] // blocks).reshape([-1 if axis == position else 1 for axis in range(len(shape))])
    return level


def noise(rng, dims, deviation, limit, pieces=(), kind=jnp.bfloat16):
    values = deviation * jax.random.normal(rng, dims, jnp.float32)
    if pieces:
        values = values * levels(rng, dims, pieces, -0.22, 0.18)
    return jnp.clip(values, -limit, limit).astype(kind)


def setup_inputs(seed: int = 0, part: int = 0) -> dict:
    arg_keys = jax.random.split(jax.random.key(seed), 4)
    part_splits = jax.random.split(jax.random.fold_in(arg_keys[3], part), 4)
    series = noise(part_splits[0], (LENGTH // 256, 256), 1.0, 6.0, ((0, 16),), jnp.float32)
    templates = noise(arg_keys[1], (TEMPLATES, 2, TAPS), (TEMPLATES * TAPS) ** -0.5, 0.125)
    drift = draw_drift(jax.random.fold_in(arg_keys[3], 71), part)
    return dict(series=series, templates=templates, drift=drift)


def kernel_matrix(templates, drift):
    tap_count = TAPS
    kernel_len = 2 * tap_count
    shifted = jnp.arange(kernel_len, dtype=jnp.int32)[None, :, None] - drift[:, None, None]
    selector = (shifted == jnp.arange(tap_count, dtype=jnp.int32)[None, None, :]).astype(jnp.float32)
    kernel = jnp.einsum('msj,mxj->mxs', selector, templates.astype(jnp.float32))
    padded = jnp.concatenate([kernel, jnp.zeros((TEMPLATES, 2, 3 * tap_count - kernel_len + 1), jnp.float32)], axis=2)
    tiled = jnp.tile(padded, (1, 1, tap_count))[:, :, :tap_count * 3 * tap_count]
    banded = tiled.reshape(TEMPLATES, 2, tap_count, 3 * tap_count)
    band_re = jnp.transpose(banded[:, 0], (2, 0, 1))
    band_im = jnp.transpose(banded[:, 1], (2, 0, 1))
    upper = jnp.stack([band_re, band_im], axis=1)
    lower = jnp.stack([-band_im, band_re], axis=1)
    return jnp.stack([upper, lower]).reshape(2 * 3 * tap_count, 2 * TEMPLATES * tap_count)

def reference(series, templates, drift):
    sample_pairs = series.reshape(-1, 2)
    signal = sample_pairs[:, 0] + 1j * sample_pairs[:, 1]
    spec_z = jnp.fft.fft(signal)
    mirrored = jnp.conj(jnp.roll(spec_z[::-1], 1))
    even_part = (spec_z + mirrored) * 0.5
    odd_part = (spec_z - mirrored) * -0.5j
    bin_ids = jnp.arange(BINS, dtype=jnp.int32)
    phase_angle = bin_ids.astype(jnp.float32) * (-2.0 * math.pi / LENGTH)
    twiddle = jnp.cos(phase_angle) + 1j * jnp.sin(phase_angle)
    real_spectrum = (even_part + twiddle * odd_part) * (1.0 / math.sqrt(LENGTH))
    spectrum = jnp.stack([jnp.real(real_spectrum), jnp.imag(real_spectrum)]).astype(jnp.bfloat16)
    row_count = BINS // TAPS
    extended = jnp.concatenate([spectrum, jnp.zeros((2, 2 * TAPS), jnp.bfloat16)], axis=1).reshape(2, row_count + 2, TAPS)
    wide_kernel = kernel_matrix(templates, drift)
    block_rows = math.gcd(row_count, 4096)

    def block_power(row_start):
        row_piece = lax.dynamic_slice_in_dim(extended, row_start, block_rows + 2, axis=1).astype(jnp.float32)
        windows = jnp.concatenate([row_piece[:, shift_idx:shift_idx + block_rows] for shift_idx in range(3)], axis=2)
        stacked = jnp.transpose(windows, (1, 0, 2)).reshape(block_rows, 6 * TAPS)
        response = jnp.dot(stacked, wide_kernel, preferred_element_type=jnp.float32, precision=lax.Precision.HIGHEST)
        return lax.optimization_barrier(jnp.sum(jnp.square(response.reshape(block_rows, 2 * TEMPLATES, TAPS)), axis=1))
    starts = jnp.arange(row_count // block_rows, dtype=jnp.int32) * block_rows
    return lax.map(block_power, starts).reshape(row_count, TAPS)
```

```python
import math

import jax
import jax.numpy as jnp
import numpy as np
from jax import lax
from jax.experimental import pallas as pl
from jax.experimental.pallas import tpu as pltpu
from jax.sharding import PartitionSpec as P

LANES = 128
AXES = ("gx", "gy")
VMEM_SPEC = pl.BlockSpec(memory_space=pltpu.VMEM)
SMEM_SPEC = pl.BlockSpec(memory_space=pltpu.SMEM)
F32 = jnp.float32
BF16 = jnp.bfloat16


def split_pair(table):
    high = np.asarray(table, np.float32).astype(BF16)
    low = (np.asarray(table, np.float64) - high.astype(np.float64)).astype(BF16)
    return high, low


def phases(product, length):
    angle = (product % length).astype(np.float64) * (-2.0 * np.pi / length)
    return np.cos(angle), np.sin(angle)


def first_matrix():
    index = np.arange(LANES, dtype=np.int64)
    real, imag = phases(index[:, None] * index[None, :], LANES)
    high, low = split_pair(np.concatenate([real, imag], axis=0))
    return np.concatenate([high, high, low], axis=1)


def second_matrix():
    index = np.arange(LANES, dtype=np.int64)
    real, imag = phases(index[:, None] * index[None, :], LANES)
    top = np.concatenate([real, -imag], axis=1)
    bottom = np.concatenate([imag, real], axis=1)
    high, low = split_pair(np.concatenate([top, bottom], axis=0))
    return np.concatenate([high, high, low], axis=1)


def table_pair(product, length):
    return np.stack(phases(product, length)).astype(np.float32)


def times(left, right):
    return (
        left[0] * right[0] - left[1] * right[1],
        left[0] * right[1] + left[1] * right[0],
    )


def small_fft(values):
    count = len(values)
    if count == 1:
        return values
    even = small_fft(values[0::2])
    odd = small_fft(values[1::2])
    head, tail = [], []
    for step in range(count // 2):
        real, imag = odd[step]
        if step == 0:
            turned = (real, imag)
        elif 4 * step == count:
            turned = (imag, -real)
        elif 8 * step == count:
            turned = ((real + imag) * math.sqrt(0.5), (imag - real) * math.sqrt(0.5))
        elif 8 * step == 3 * count:
            turned = ((imag - real) * math.sqrt(0.5), (real + imag) * -math.sqrt(0.5))
        else:
            angle = -2.0 * math.pi * step / count
            cosine, sine = math.cos(angle), math.sin(angle)
            turned = (real * cosine - imag * sine, real * sine + imag * cosine)
        head.append((even[step][0] + turned[0], even[step][1] + turned[1]))
        tail.append((even[step][0] - turned[0], even[step][1] - turned[1]))
    return head + tail


def powered(first, count):
    powers = [None, first]
    for step in range(2, count):
        half = step // 2
        powers.append(times(powers[half], powers[step - half]))
    return powers


def columns_kernel(groups, series_ref, out_ref, turned):
    rows, width = series_ref.shape
    per_row = width // groups
    tall = rows // LANES
    for high in range(tall):
        turned[...] = series_ref[high * LANES : (high + 1) * LANES, :].T
        for dest in range(groups):
            out_ref[dest, pl.ds(high, per_row, stride=tall), :] = turned[
                pl.ds(dest, per_row, stride=groups), :
            ]


def spread_samples(series, groups):
    rows, width = series.shape
    per_row = width // groups
    inner = rows * width // (LANES * LANES)
    tall = LANES // groups
    if per_row == inner:
        return pl.pallas_call(
            lambda *refs: columns_kernel(groups, *refs),
            out_shape=jax.ShapeDtypeStruct((groups, inner * tall, LANES), F32),
            in_specs=[VMEM_SPEC],
            out_specs=VMEM_SPEC,
            scratch_shapes=[pltpu.VMEM((width, LANES), F32)],
        )(series)
    shaped = series.reshape(tall, LANES, inner // per_row, per_row, groups)
    return jnp.transpose(shaped, (4, 2, 3, 0, 1)).reshape(groups, inner * tall, LANES)


def local_kernel(groups, y_ref, w1_ref, w2_ref, t1_ref, t2_ref, out_ref, rhs, lhs, mid, bins, edge):
    inner = mid.shape[0]
    tall = y_ref.shape[1] // inner
    own = out_ref.shape[1] // 2 - 4
    for pair in range(inner // 2):
        for part in range(2):
            step = 2 * pair + part
            block = y_ref[:, step * tall : (step + 1) * tall, :].reshape(LANES, LANES)
            high = block.astype(BF16)
            low = (block - high.astype(F32)).astype(BF16)
            cols = slice(part * LANES, (part + 1) * LANES)
            rhs[0:LANES, cols] = high
            rhs[LANES : 2 * LANES, cols] = low
            rhs[2 * LANES : 3 * LANES, cols] = high
        first = jnp.dot(w1_ref[...], rhs[...], preferred_element_type=F32)
        for part in range(2):
            cols = slice(part * LANES, (part + 1) * LANES)
            turned = times(
                (first[:LANES, cols], first[LANES:, cols]), (t1_ref[0], t1_ref[1])
            )
            rows = slice(part * LANES, (part + 1) * LANES)
            for comp in range(2):
                high = turned[comp].astype(BF16)
                low = (turned[comp] - high.astype(F32)).astype(BF16)
                at = comp * LANES
                lhs[rows, at : at + LANES] = high
                lhs[rows, 2 * LANES + at : 3 * LANES + at] = low
                lhs[rows, 4 * LANES + at : 5 * LANES + at] = high
        second = lax.dot_general(
            w2_ref[...], lhs[...], (((1,), (1,)), ((), ())), preferred_element_type=F32
        )
        mid[2 * pair] = second[:, :LANES]
        mid[2 * pair + 1] = second[:, LANES:]

    def combine(chunk, carry):
        rows = pl.ds(pl.multiple_of(chunk * 8, 8), 8)
        rows_im = pl.ds(pl.multiple_of(LANES + chunk * 8, 8), 8)
        powers = powered((t2_ref[0, rows, :], t2_ref[1, rows, :]), inner)
        values = [(mid[0, rows, :], mid[0, rows_im, :])]
        for step in range(1, inner):
            values.append(times((mid[step, rows, :], mid[step, rows_im, :]), powers[step]))
        result = small_fft(values)
        for comp in range(2):
            for step in range(inner // 2):
                at = pl.multiple_of(8 + step * LANES + chunk * 8, 8)
                bins[comp, pl.ds(at, 8), :] = result[step][comp]
            edge[comp, rows, :] = result[inner // 2][comp]
            edge[2 + comp, rows, :] = result[inner - 1][comp]
        return carry

    lax.fori_loop(0, LANES // 8, combine, 0)
    total = inner // 2 * LANES
    for comp in range(2):
        bins[comp, 0:8, :] = edge[2 + comp, LANES - 8 : LANES, :]
        bins[comp, 8 + total : 16 + total, :] = edge[comp, 0:8, :]
    for dest in range(groups):
        base = 8 + own * dest
        for comp in range(2):
            out_ref[dest, comp * own : (comp + 1) * own, :] = bins[comp, base : base + own, :]
            at = 2 * own + 4 * comp
            out_ref[dest, at : at + 2, :] = bins[comp, base - 2 : base, :]
            out_ref[dest, at + 2 : at + 4, :] = bins[comp, base + own : base + own + 2, :]


def local_transform(moved, groups, w1, w2, t1, t2):
    inner = moved.shape[1] * groups // LANES
    total = inner // 2 * LANES
    own = total // groups
    return pl.pallas_call(
        lambda *refs: local_kernel(groups, *refs),
        out_shape=jax.ShapeDtypeStruct((groups, 2 * own + 8, LANES), F32),
        in_specs=[VMEM_SPEC] * 5,
        out_specs=VMEM_SPEC,
        scratch_shapes=[
            pltpu.VMEM((3 * LANES, 2 * LANES), BF16),
            pltpu.VMEM((2 * LANES, 6 * LANES), BF16),
            pltpu.VMEM((inner, 2 * LANES, LANES), F32),
            pltpu.VMEM((2, total + 16, LANES), F32),
            pltpu.VMEM((4, LANES, LANES), F32),
        ],
    )(moved, w1, w2, t1, t2)


def matrix_kernel(drift_ref, taps_ref, out_ref):
    row = lax.broadcasted_iota(jnp.int32, (LANES, LANES), 0)
    col = lax.broadcasted_iota(jnp.int32, (LANES, LANES), 1)
    below = col <= row
    lag = (row - col) & (LANES - 1)

    def build(index, carry):
        shift = drift_ref[index]
        late = lag >= shift
        lane = lax.broadcasted_iota(jnp.int32, (8, LANES), 1)
        source = (-lane - shift) & (LANES - 1)
        blocks = []
        for comp in range(2):
            taps = jnp.broadcast_to(taps_ref[index, pl.ds(comp, 1), :].astype(F32), (8, LANES))
            start = jnp.take_along_axis(taps, source, axis=1)
            start = jnp.broadcast_to(start[0:1, :], (LANES, LANES))
            ring = pltpu.roll(start, 0, 1, stride=1, stride_axis=0)
            low = jnp.where(late, ring, 0.0)
            high = jnp.where(late, 0.0, ring)
            blocks.append(
                (
                    jnp.where(below, low, 0.0),
                    jnp.where(below, high, low),
                    jnp.where(below, 0.0, high),
                )
            )
        for part in range(3):
            real, imag = blocks[0][part], blocks[1][part]
            top = slice(part * LANES, (part + 1) * LANES)
            bottom = slice((3 + part) * LANES, (4 + part) * LANES)
            out_ref[index, top, 0:LANES] = real.astype(BF16)
            out_ref[index, top, LANES:] = imag.astype(BF16)
            out_ref[index, bottom, 0:LANES] = (-imag).astype(BF16)
            out_ref[index, bottom, LANES:] = real.astype(BF16)
        return carry

    lax.fori_loop(0, taps_ref.shape[0], build, 0)


def template_matrices(templates, drift):
    count = templates.shape[0]
    return pl.pallas_call(
        matrix_kernel,
        out_shape=jax.ShapeDtypeStruct((count, 6 * LANES, 2 * LANES), BF16),
        in_specs=[SMEM_SPEC, VMEM_SPEC],
        out_specs=VMEM_SPEC,
        cost_estimate=pl.CostEstimate(
            flops=count * 40 * LANES * LANES,
            bytes_accessed=count * 24 * LANES * LANES,
            transcendentals=0,
        ),
    )(drift, templates)


def power_kernel(groups, scale, place_ref, z_ref, table_ref, w_ref, out_ref, bins, lhs):
    own = z_ref.shape[1] // 2 - 4
    half = groups // 2

    def combine(chunk, carry):
        rows = pl.ds(pl.multiple_of(chunk * 8, 8), 8)
        rows_im = pl.ds(pl.multiple_of(own + chunk * 8, 8), 8)
        at = pl.ds(pl.multiple_of(8 + chunk * 8, 8), 8)
        powers = powered((table_ref[0, at, :], table_ref[1, at, :]), groups)
        values = [(z_ref[0, rows, :], z_ref[0, rows_im, :])]
        for step in range(1, groups):
            values.append(times((z_ref[step, rows, :], z_ref[step, rows_im, :]), powers[step]))
        result = small_fft(values)
        for step in range(groups):
            sign = scale if step < half else -scale
            bins[step, 0, at, :] = result[step][0] * scale
            bins[step, 1, at, :] = result[step][1] * sign
        return carry

    lax.fori_loop(0, own // 8, combine, 0)
    rim = []
    for comp in range(2):
        rim.append(
            jnp.concatenate(
                [
                    table_ref[comp, 6:8, :],
                    table_ref[comp, 8 + own : 10 + own, :],
                    table_ref[comp, 6:8, :],
                    table_ref[comp, 8 + own : 10 + own, :],
                ]
            )
        )
    powers = powered((rim[0], rim[1]), groups)
    values = []
    for step in range(groups):
        both = z_ref[step, 2 * own : 2 * own + 8, :]
        value = (both, pltpu.roll(both, 4, 0))
        values.append(times(value, powers[step]) if step else value)
    result = small_fft(values)
    for step in range(groups):
        sign = scale if step < half else -scale
        for comp in range(2):
            value = result[step][comp] * (sign if comp else scale)
            bins[step, comp, 6:8, :] = value[0:2, :]
            bins[step, comp, 8 + own : 10 + own, :] = value[2:4, :]

    lane = lax.broadcasted_iota(jnp.int32, (8, LANES), 1)
    source = (LANES - lane) & (LANES - 1)
    rank = lax.broadcasted_iota(jnp.int32, (8, LANES), 0)
    for step in range(half, groups):
        for comp in range(2):
            for chunk in range(own // 8 + 1):
                here = bins[step, comp, 8 * chunk : 8 * chunk + 8, :]
                after = bins[step, comp, 8 * chunk + 1 : 8 * chunk + 9, :]
                value = jnp.where(lane == 0, after, jnp.take_along_axis(here, source, axis=1))
                if step == half and chunk == 0:
                    value = jnp.where(place_ref[0] == 0, 0.0, value)
                bins[step, comp, 8 * chunk : 8 * chunk + 8, :] = value
    for step in range(groups):
        for comp in range(2):
            for shift in range(3):
                at = 8 + shift if step < half else 8 - shift
                cols = slice((3 * comp + shift) * LANES, (3 * comp + shift + 1) * LANES)
                lhs[step * own : (step + 1) * own, cols] = bins[
                    step, comp, at : at + own, :
                ].astype(BF16)

    piece = min(256, groups * own)
    out_ref[...] = jnp.zeros_like(out_ref)

    def template(index, carry):
        for block in range(groups * own // piece):
            rows = slice(block * piece, (block + 1) * piece)
            response = jnp.dot(lhs[rows, :], w_ref[index], preferred_element_type=F32)
            power = response[:, :LANES] * response[:, :LANES]
            power = power + response[:, LANES:] * response[:, LANES:]
            out_ref[rows, :] += power
        return carry

    lax.fori_loop(0, w_ref.shape[0], template, 0)


def template_powers(place, moved, table, matrices, scale):
    groups = moved.shape[0]
    own = moved.shape[1] // 2 - 4
    return pl.pallas_call(
        lambda *refs: power_kernel(groups, scale, *refs),
        out_shape=jax.ShapeDtypeStruct((groups * own, LANES), F32),
        in_specs=[SMEM_SPEC, VMEM_SPEC, VMEM_SPEC, VMEM_SPEC],
        out_specs=VMEM_SPEC,
        scratch_shapes=[
            pltpu.VMEM((groups, 2, own + 24, LANES), F32),
            pltpu.VMEM((groups * own, 6 * LANES), BF16),
        ],
    )(place, moved, table, matrices)


def place_kernel(place_ref, power_ref, out_ref):
    groups, own = power_ref.shape[0], power_ref.shape[1]
    total = groups * own
    flip = 7 - lax.broadcasted_iota(jnp.int32, (8, LANES), 0)

    @pl.when(place_ref[0] % 2 == 0)
    def _():
        for source in range(groups):
            out_ref[source * own : (source + 1) * own, :] = power_ref[source]

    @pl.when(place_ref[0] % 2 == 1)
    def _():
        for source in range(groups):
            for chunk in range(own // 8):
                at = total - source * own - 8 * chunk - 8
                value = power_ref[source, 8 * chunk : 8 * chunk + 8, :]
                out_ref[at : at + 8, :] = jnp.take_along_axis(value, flip, axis=0)


def place_powers(place, moved):
    groups, own = moved.shape[0], moved.shape[1]
    return pl.pallas_call(
        place_kernel,
        out_shape=jax.ShapeDtypeStruct((groups * own, LANES), F32),
        in_specs=[SMEM_SPEC, VMEM_SPEC],
        out_specs=VMEM_SPEC,
    )(place, moved)


def exchange(value):
    return lax.all_to_all(value, AXES, split_axis=0, concat_axis=0, tiled=True)


def body(series, templates, drift):
    groups = lax.axis_size(AXES)
    place = lax.axis_index(AXES)
    samples = series.shape[0] * series.shape[1]
    length = samples * groups
    inner = samples // (LANES * LANES)
    total = inner // 2 * LANES
    own = total // groups
    index = np.arange(LANES, dtype=np.int64)
    w1 = jnp.asarray(first_matrix())
    w2 = jnp.asarray(second_matrix())
    t1 = jnp.asarray(table_pair(index[:, None] * index[None, :], LANES * LANES))
    t2 = jnp.asarray(table_pair(LANES * index[:, None] + index[None, :], samples))
    rows = np.arange(-8, total + 8, dtype=np.int64)
    wide = jnp.asarray(table_pair(LANES * rows[:, None] + index[None, :], length))
    table = lax.dynamic_slice_in_dim(wide, place * own, own + 16, axis=1)
    place = place.astype(jnp.int32).reshape(1)

    matrices = template_matrices(templates, drift)
    moved = exchange(spread_samples(series, groups))
    partial = local_transform(moved, groups, w1, w2, t1, t2)
    moved = exchange(partial)
    power = template_powers(place, moved, table, matrices, 1.0 / math.sqrt(length))
    power = power.reshape(groups, own, LANES)
    half = groups // 2
    paired = jnp.stack([power[:half], power[half:][::-1]], axis=1)
    return place_powers(place, exchange(paired.reshape(groups, own, LANES)))


def solution(mesh):
    in_specs = (P(("band", "gx", "gy"), None), P(), P())
    out_specs = P(("band", "gx", "gy"), None)
    return jax.shard_map(body, mesh=mesh, in_specs=in_specs, out_specs=out_specs, check_vma=False)
```

```python
import math

import jax
import jax.numpy as jnp
import numpy as np
from jax import lax
from jax.experimental import pallas as pl
from jax.experimental.pallas import tpu as pltpu
from jax.sharding import PartitionSpec as P

LANES = 128
AXES = ("gx", "gy")
VMEM_SPEC = pl.BlockSpec(memory_space=pltpu.VMEM)
SMEM_SPEC = pl.BlockSpec(memory_space=pltpu.SMEM)
F32 = jnp.float32
F16 = jnp.float16
STEPS = (64, 32, 16, 8, 4, 2, 1)
PEAK = 2.0**14
REACH = 2.0**-40
BF16 = jnp.bfloat16


def split_pair(table):
    high = np.asarray(table, np.float32).astype(BF16)
    low = (np.asarray(table, np.float64) - high.astype(np.float64)).astype(BF16)
    return high, low


def phases(product, length):
    angle = (product % length).astype(np.float64) * (-2.0 * np.pi / length)
    return np.cos(angle), np.sin(angle)


def first_matrix():
    index = np.arange(LANES, dtype=np.int64)
    real, imag = phases(index[:, None] * index[None, :], LANES)
    high, low = split_pair(np.concatenate([real, imag], axis=0))
    return np.concatenate([high, high, low], axis=1)


def second_matrix(gain):
    index = np.arange(LANES, dtype=np.int64)
    real, imag = phases(index[:, None] * index[None, :], LANES)
    real, imag = real * gain, imag * gain
    top = np.concatenate([real, -imag], axis=1)
    bottom = np.concatenate([imag, real], axis=1)
    high, low = split_pair(np.concatenate([top, bottom], axis=0))
    return np.concatenate([high, high, low], axis=1)


def table_pair(product, length):
    return np.stack(phases(product, length)).astype(np.float32)


def times(left, right):
    return (
        left[0] * right[0] - left[1] * right[1],
        left[0] * right[1] + left[1] * right[0],
    )


def small_fft(values):
    count = len(values)
    if count == 1:
        return values
    even = small_fft(values[0::2])
    odd = small_fft(values[1::2])
    head, tail = [], []
    for step in range(count // 2):
        real, imag = odd[step]
        if step == 0:
            turned = (real, imag)
        elif 4 * step == count:
            turned = (imag, -real)
        elif 8 * step == count:
            turned = ((real + imag) * math.sqrt(0.5), (imag - real) * math.sqrt(0.5))
        elif 8 * step == 3 * count:
            turned = ((imag - real) * math.sqrt(0.5), (real + imag) * -math.sqrt(0.5))
        else:
            angle = -2.0 * math.pi * step / count
            cosine, sine = math.cos(angle), math.sin(angle)
            turned = (real * cosine - imag * sine, real * sine + imag * cosine)
        head.append((even[step][0] + turned[0], even[step][1] + turned[1]))
        tail.append((even[step][0] - turned[0], even[step][1] - turned[1]))
    return head + tail


def powered(first, count):
    powers = [None, first]
    for step in range(2, count):
        half = step // 2
        powers.append(times(powers[half], powers[step - half]))
    return powers


def grow(peak, scale):
    code = 0.0
    for step in STEPS:
        grown = scale * 2.0**step
        fits = peak * grown <= PEAK
        scale = jnp.where(fits, grown, scale)
        code = jnp.where(fits, code + step, code)
    return scale, code


def shrink(code, scale):
    factor = jnp.full(code.shape, scale, F32)
    for step in STEPS:
        taken = code >= step
        factor = jnp.where(taken, factor * 2.0**-step, factor)
        code = jnp.where(taken, code - step, code)
    return factor


def columns_kernel(groups, series_ref, out_ref, turned):
    rows, width = series_ref.shape
    scale, code = grow(jnp.max(jnp.abs(series_ref[...])), 1.0)
    inner = out_ref.shape[1] - 8
    for dest in range(groups):
        out_ref[dest, inner : inner + 8, :] = jnp.full((8, LANES), code, F32)
    per_row = width // groups
    tall = rows // LANES
    for high in range(tall):
        turned[...] = (series_ref[high * LANES : (high + 1) * LANES, :] * scale).T
        for dest in range(groups):
            out_ref[dest, pl.ds(high, per_row, stride=tall), :] = turned[
                pl.ds(dest, per_row, stride=groups), :
            ]


def spread_samples(series, groups):
    rows, width = series.shape
    per_row = width // groups
    inner = rows * width // (LANES * LANES)
    tall = LANES // groups
    if per_row == inner:
        return pl.pallas_call(
            lambda *refs: columns_kernel(groups, *refs),
            out_shape=jax.ShapeDtypeStruct((groups, inner * tall + 8, LANES), F32),
            in_specs=[VMEM_SPEC],
            out_specs=VMEM_SPEC,
            scratch_shapes=[pltpu.VMEM((width, LANES), F32)],
        )(series)
    scale, code = grow(jnp.max(jnp.abs(series)), F32(1.0))
    shaped = (series * scale).reshape(tall, LANES, inner // per_row, per_row, groups)
    moving = jnp.transpose(shaped, (4, 2, 3, 0, 1)).reshape(groups, inner * tall, LANES)
    return jnp.concatenate([moving, jnp.full((groups, 8, LANES), code, F32)], axis=1)


def local_kernel(
    groups, unit, y_ref, w1_ref, w2_ref, t1_ref, t2_ref, out_ref, level_ref, rhs, lhs, mid, bins, edge
):
    inner = mid.shape[0]
    taken = y_ref.shape[1] - 8
    tall = taken // inner
    own = out_ref.shape[1] // 2 - 4
    codes = y_ref[:, taken:, :]
    least = jnp.min(codes, axis=0)
    level_ref[...] = shrink(least, unit)
    factor = shrink(codes - least[None], 1.0)
    factor = factor[:, :tall, :] if tall <= 8 else factor[:, :1, :]
    for pair in range(inner // 2):
        for part in range(2):
            step = 2 * pair + part
            block = y_ref[:, step * tall : (step + 1) * tall, :] * factor
            block = block.reshape(LANES, LANES)
            high = block.astype(BF16)
            low = (block - high.astype(F32)).astype(BF16)
            cols = slice(part * LANES, (part + 1) * LANES)
            rhs[0:LANES, cols] = high
            rhs[LANES : 2 * LANES, cols] = low
            rhs[2 * LANES : 3 * LANES, cols] = high
        first = jnp.dot(w1_ref[...], rhs[...], preferred_element_type=F32)
        for part in range(2):
            cols = slice(part * LANES, (part + 1) * LANES)
            turned = times(
                (first[:LANES, cols], first[LANES:, cols]), (t1_ref[0], t1_ref[1])
            )
            rows = slice(part * LANES, (part + 1) * LANES)
            for comp in range(2):
                high = turned[comp].astype(BF16)
                low = (turned[comp] - high.astype(F32)).astype(BF16)
                at = comp * LANES
                lhs[rows, at : at + LANES] = high
                lhs[rows, 2 * LANES + at : 3 * LANES + at] = low
                lhs[rows, 4 * LANES + at : 5 * LANES + at] = high
        second = lax.dot_general(
            w2_ref[...], lhs[...], (((1,), (1,)), ((), ())), preferred_element_type=F32
        )
        mid[2 * pair] = second[:, :LANES]
        mid[2 * pair + 1] = second[:, LANES:]

    def combine(chunk, carry):
        rows = pl.ds(pl.multiple_of(chunk * 8, 8), 8)
        rows_im = pl.ds(pl.multiple_of(LANES + chunk * 8, 8), 8)
        powers = powered((t2_ref[0, rows, :], t2_ref[1, rows, :]), inner)
        values = [(mid[0, rows, :], mid[0, rows_im, :])]
        for step in range(1, inner):
            values.append(times((mid[step, rows, :], mid[step, rows_im, :]), powers[step]))
        result = small_fft(values)
        for comp in range(2):
            for step in range(inner // 2):
                at = pl.multiple_of(8 + step * LANES + chunk * 8, 8)
                bins[comp, pl.ds(at, 8), :] = result[step][comp]
            edge[comp, rows, :] = result[inner // 2][comp]
            edge[2 + comp, rows, :] = result[inner - 1][comp]
        return carry

    lax.fori_loop(0, LANES // 8, combine, 0)
    total = inner // 2 * LANES
    for comp in range(2):
        bins[comp, 0:8, :] = edge[2 + comp, LANES - 8 : LANES, :]
        bins[comp, 8 + total : 16 + total, :] = edge[comp, 0:8, :]
    for dest in range(groups):
        base = 8 + own * dest
        for comp in range(2):
            out_ref[dest, comp * own : (comp + 1) * own, :] = bins[comp, base : base + own, :]
            at = 2 * own + 4 * comp
            out_ref[dest, at : at + 2, :] = bins[comp, base - 2 : base, :]
            out_ref[dest, at + 2 : at + 4, :] = bins[comp, base + own : base + own + 2, :]


def local_transform(moved, groups, unit, w1, w2, t1, t2):
    inner = (moved.shape[1] - 8) * groups // LANES
    total = inner // 2 * LANES
    own = total // groups
    return pl.pallas_call(
        lambda *refs: local_kernel(groups, unit, *refs),
        out_shape=(
            jax.ShapeDtypeStruct((groups, 2 * own + 8, LANES), F32),
            jax.ShapeDtypeStruct((8, LANES), F32),
        ),
        in_specs=[VMEM_SPEC] * 5,
        out_specs=(VMEM_SPEC, VMEM_SPEC),
        scratch_shapes=[
            pltpu.VMEM((3 * LANES, 2 * LANES), BF16),
            pltpu.VMEM((2 * LANES, 6 * LANES), BF16),
            pltpu.VMEM((inner, 2 * LANES, LANES), F32),
            pltpu.VMEM((2, total + 16, LANES), F32),
            pltpu.VMEM((4, LANES, LANES), F32),
        ],
    )(moved, w1, w2, t1, t2)


def matrix_kernel(taps_ref, out_ref):
    row = lax.broadcasted_iota(jnp.int32, (LANES, LANES), 0)
    col = lax.broadcasted_iota(jnp.int32, (LANES, LANES), 1)
    below = col <= row

    def build(index, carry):
        lane = lax.broadcasted_iota(jnp.int32, (8, LANES), 1)
        source = (LANES - lane) & (LANES - 1)
        blocks = []
        for comp in range(2):
            taps = jnp.broadcast_to(taps_ref[index, pl.ds(comp, 1), :].astype(F32), (8, LANES))
            start = jnp.take_along_axis(taps, source, axis=1)
            start = jnp.broadcast_to(start[0:1, :], (LANES, LANES))
            ring = pltpu.roll(start, 0, 1, stride=1, stride_axis=0)
            blocks.append((jnp.where(below, ring, 0.0), jnp.where(below, 0.0, ring)))
        for part in range(2):
            real, imag = blocks[0][part], blocks[1][part]
            top = slice(part * LANES, (part + 1) * LANES)
            bottom = slice((2 + part) * LANES, (3 + part) * LANES)
            out_ref[index, top, 0:LANES] = real.astype(BF16)
            out_ref[index, top, LANES:] = imag.astype(BF16)
            out_ref[index, bottom, 0:LANES] = (-imag).astype(BF16)
            out_ref[index, bottom, LANES:] = real.astype(BF16)
        return carry

    lax.fori_loop(0, taps_ref.shape[0], build, 0)


def template_matrices(templates):
    count = templates.shape[0]
    return pl.pallas_call(
        matrix_kernel,
        out_shape=jax.ShapeDtypeStruct((count, 4 * LANES, 2 * LANES), BF16),
        in_specs=[VMEM_SPEC],
        out_specs=VMEM_SPEC,
        cost_estimate=pl.CostEstimate(
            flops=count * 40 * LANES * LANES,
            bytes_accessed=count * 24 * LANES * LANES,
            transcendentals=0,
        ),
    )(templates)


def power_kernel(
    place_ref, drift_ref, z_ref, level_ref, table_ref, w_ref, out_ref, bins, rim_rows, lhs, near, far
):
    groups = z_ref.shape[0]
    own = z_ref.shape[1] // 2 - 4
    half = groups // 2
    main = groups * own
    scale = level_ref[...]

    def combine(chunk, carry):
        rows = pl.ds(pl.multiple_of(chunk * 8, 8), 8)
        rows_im = pl.ds(pl.multiple_of(own + chunk * 8, 8), 8)
        at = pl.ds(pl.multiple_of(8 + chunk * 8, 8), 8)
        powers = powered((table_ref[0, at, :], table_ref[1, at, :]), groups)
        values = [(z_ref[0, rows, :], z_ref[0, rows_im, :])]
        for step in range(1, groups):
            values.append(times((z_ref[step, rows, :], z_ref[step, rows_im, :]), powers[step]))
        result = small_fft(values)
        for step in range(groups):
            sign = level_ref[...] if step < half else -level_ref[...]
            bins[step, 0, at, :] = result[step][0] * level_ref[...]
            bins[step, 1, at, :] = result[step][1] * sign
        return carry

    lax.fori_loop(0, own // 8, combine, 0)
    rim = []
    for comp in range(2):
        rim.append(
            jnp.concatenate(
                [
                    table_ref[comp, 6:8, :],
                    table_ref[comp, 8 + own : 10 + own, :],
                    table_ref[comp, 6:8, :],
                    table_ref[comp, 8 + own : 10 + own, :],
                ]
            )
        )
    powers = powered((rim[0], rim[1]), groups)
    values = []
    for step in range(groups):
        both = z_ref[step, 2 * own : 2 * own + 8, :]
        value = (both, pltpu.roll(both, 4, 0))
        values.append(times(value, powers[step]) if step else value)
    result = small_fft(values)
    for step in range(groups):
        sign = scale if step < half else -scale
        for comp in range(2):
            value = result[step][comp] * (sign if comp else scale)
            bins[step, comp, 6:8, :] = value[0:2, :]
            bins[step, comp, 8 + own : 10 + own, :] = value[2:4, :]

    lane = lax.broadcasted_iota(jnp.int32, (8, LANES), 1)
    source = (LANES - lane) & (LANES - 1)
    rank = lax.broadcasted_iota(jnp.int32, (8, LANES), 0)
    for step in range(half, groups):
        for comp in range(2):
            for chunk in range(own // 8 + 1):
                here = bins[step, comp, 8 * chunk : 8 * chunk + 8, :]
                after = bins[step, comp, 8 * chunk + 1 : 8 * chunk + 9, :]
                value = jnp.where(lane == 0, after, jnp.take_along_axis(here, source, axis=1))
                if step == half and chunk == 0:
                    value = jnp.where(place_ref[0] == 0, 0.0, value)
                bins[step, comp, 8 * chunk : 8 * chunk + 8, :] = value
    for step in range(groups):
        for comp in range(2):
            for shift in range(2):
                at = 8 + shift if step < half else 8 - shift
                cols = slice((2 * comp + shift) * LANES, (2 * comp + shift + 1) * LANES)
                lhs[step * own : (step + 1) * own, cols] = bins[
                    step, comp, at : at + own, :
                ].astype(BF16)
                at = 8 + own + shift if step < half else 7 - shift
                rim_rows[2 * comp + shift, step : step + 1, :] = bins[step, comp, at : at + 1, :]
    for part in range(4):
        lhs[main:, part * LANES : (part + 1) * LANES] = rim_rows[part].astype(BF16)

    near[...] = jnp.zeros_like(near)
    far[...] = jnp.zeros_like(far)
    pieces = max(1, main // 512)
    edges = [main // pieces * piece for piece in range(pieces)] + [main + groups]

    def template(index, carry):
        shift = drift_ref[index]
        for piece in range(pieces):
            rows = slice(edges[piece], edges[piece + 1])
            response = jnp.dot(lhs[rows, :], w_ref[index], preferred_element_type=F32)
            power = response[:, :LANES] * response[:, :LANES]
            power = power + response[:, LANES:] * response[:, LANES:]
            rolled = pltpu.roll(power, (LANES - shift) & (LANES - 1), 1)
            inside = lax.broadcasted_iota(jnp.int32, rolled.shape, 1) < LANES - shift
            near[rows, :] += jnp.where(inside, rolled, 0.0)
            far[rows, :] += jnp.where(inside, 0.0, rolled)
        return carry

    lax.fori_loop(0, w_ref.shape[0], template, 0)
    peak = jnp.zeros((8, LANES), F32)
    for step in range(groups):
        base = step * own
        spare = far[main + step : main + step + 1, :]
        if step < half:
            dest = 2 * step
            out_ref[dest, 0:own, :] = near[base : base + own, :] + far[base + 1 : base + own + 1, :]
            out_ref[dest, own - 1 : own, :] = near[base + own - 1 : base + own, :] + spare
        else:
            dest = 2 * (groups - 1 - step) + 1
            out_ref[dest, 0:own, :] = near[base : base + own, :] + far[base - 1 : base + own - 1, :]
            out_ref[dest, 0:1, :] = near[base : base + 1, :] + spare
        for chunk in range(own // 8):
            peak = jnp.maximum(peak, out_ref[dest, 8 * chunk : 8 * chunk + 8, :])
    scale, code = grow(jnp.max(peak), REACH)
    for dest in range(groups):
        out_ref[dest, 0:own, :] = out_ref[dest, 0:own, :] * scale
        out_ref[dest, own : own + 8, :] = jnp.full((8, LANES), code, F32)


def template_powers(place, drift, moved, level, table, matrices):
    groups = moved.shape[0]
    own = moved.shape[1] // 2 - 4
    rows = groups * own + groups
    return pl.pallas_call(
        power_kernel,
        out_shape=jax.ShapeDtypeStruct((groups, own + 8, LANES), F32),
        in_specs=[SMEM_SPEC, SMEM_SPEC] + [VMEM_SPEC] * 4,
        out_specs=VMEM_SPEC,
        scratch_shapes=[
            pltpu.VMEM((groups, 2, own + 24, LANES), F32),
            pltpu.VMEM((4, groups, LANES), F32),
            pltpu.VMEM((rows, 4 * LANES), BF16),
            pltpu.VMEM((rows, LANES), F32),
            pltpu.VMEM((rows, LANES), F32),
        ],
    )(place, drift, moved, level, table, matrices)


def place_kernel(place_ref, power_ref, out_ref):
    groups, own = power_ref.shape[0], power_ref.shape[1] - 8
    total = groups * own
    flip = 7 - lax.broadcasted_iota(jnp.int32, (8, LANES), 0)

    @pl.when(place_ref[0] % 2 == 0)
    def _():
        for source in range(groups):
            factor = shrink(power_ref[source, own:, :], 1.0 / REACH)
            for chunk in range(own // 8):
                at = source * own + 8 * chunk
                value = power_ref[source, 8 * chunk : 8 * chunk + 8, :] * factor
                out_ref[at : at + 8, :] = value

    @pl.when(place_ref[0] % 2 == 1)
    def _():
        for source in range(groups):
            factor = shrink(power_ref[source, own:, :], 1.0 / REACH)
            for chunk in range(own // 8):
                at = total - source * own - 8 * chunk - 8
                value = power_ref[source, 8 * chunk : 8 * chunk + 8, :] * factor
                out_ref[at : at + 8, :] = jnp.take_along_axis(value, flip, axis=0)


def place_powers(place, moved):
    groups, own = moved.shape[0], moved.shape[1] - 8
    return pl.pallas_call(
        place_kernel,
        out_shape=jax.ShapeDtypeStruct((groups * own, LANES), F32),
        in_specs=[SMEM_SPEC, VMEM_SPEC],
        out_specs=VMEM_SPEC,
    )(place, moved)


def exchange(value):
    moved = lax.all_to_all(value.astype(F16), AXES, split_axis=0, concat_axis=0, tiled=True)
    return moved.astype(F32)


def body(series, templates, drift):
    groups = lax.axis_size(AXES)
    place = lax.axis_index(AXES)
    samples = series.shape[0] * series.shape[1]
    length = samples * groups
    inner = samples // (LANES * LANES)
    total = inner // 2 * LANES
    own = total // groups
    index = np.arange(LANES, dtype=np.int64)
    w1 = jnp.asarray(first_matrix())
    w2 = jnp.asarray(second_matrix(2.0 / samples))
    t1 = jnp.asarray(table_pair(index[:, None] * index[None, :], LANES * LANES))
    t2 = jnp.asarray(table_pair(LANES * index[:, None] + index[None, :], samples))
    rows = np.arange(-8, total + 8, dtype=np.int64)
    wide = jnp.asarray(table_pair(LANES * rows[:, None] + index[None, :], length))
    table = lax.dynamic_slice_in_dim(wide, place * own, own + 16, axis=1)
    place = place.astype(jnp.int32).reshape(1)

    matrices = template_matrices(templates)
    moved = exchange(spread_samples(series, groups))
    unit = samples / 2 / math.sqrt(length)
    partial, level = local_transform(moved, groups, unit, w1, w2, t1, t2)
    moved = exchange(partial)
    power = template_powers(place, drift, moved, level, table, matrices)
    return place_powers(place, exchange(power))


def solution(mesh):
    in_specs = (P(("band", "gx", "gy"), None), P(), P())
    out_specs = P(("band", "gx", "gy"), None)
    return jax.shard_map(body, mesh=mesh, in_specs=in_specs, out_specs=out_specs, check_vma=False)
```

```python
import math

import jax
import jax.numpy as jnp
import numpy as np
from jax import lax
from jax.experimental import pallas as pl
from jax.experimental.pallas import tpu as pltpu
from jax.sharding import PartitionSpec as P

LANES = 128
AXES = ("gx", "gy")
VMEM_SPEC = pl.BlockSpec(memory_space=pltpu.VMEM)
SMEM_SPEC = pl.BlockSpec(memory_space=pltpu.SMEM)
F32 = jnp.float32
F16 = jnp.float16
STEPS = (64, 32, 16, 8, 4, 2, 1)
PEAK = 2.0**14
REACH = 2.0**-40
ROOM = pltpu.CompilerParams(vmem_limit_bytes=20 * 2**20)
BF16 = jnp.bfloat16


def split_pair(table):
    high = np.asarray(table, np.float32).astype(BF16)
    low = (np.asarray(table, np.float64) - high.astype(np.float64)).astype(BF16)
    return high, low


def phases(product, length):
    angle = (product % length).astype(np.float64) * (-2.0 * np.pi / length)
    return np.cos(angle), np.sin(angle)


def first_matrix():
    index = np.arange(LANES, dtype=np.int64)
    real, imag = phases(index[:, None] * index[None, :], LANES)
    high, low = split_pair(np.concatenate([real, imag], axis=0))
    return np.concatenate([high, high, low], axis=1)


def second_matrix(gain):
    index = np.arange(LANES, dtype=np.int64)
    real, imag = phases(index[:, None] * index[None, :], LANES)
    real, imag = real * gain, imag * gain
    top = np.concatenate([real, -imag], axis=1)
    bottom = np.concatenate([imag, real], axis=1)
    high, low = split_pair(np.concatenate([top, bottom], axis=0))
    return np.concatenate([high, high, low], axis=1)


def table_pair(product, length):
    return np.stack(phases(product, length)).astype(np.float32)


def times(left, right):
    return (
        left[0] * right[0] - left[1] * right[1],
        left[0] * right[1] + left[1] * right[0],
    )


def small_fft(values):
    count = len(values)
    if count == 1:
        return values
    even = small_fft(values[0::2])
    odd = small_fft(values[1::2])
    head, tail = [], []
    for step in range(count // 2):
        real, imag = odd[step]
        if step == 0:
            turned = (real, imag)
        elif 4 * step == count:
            turned = (imag, -real)
        elif 8 * step == count:
            turned = ((real + imag) * math.sqrt(0.5), (imag - real) * math.sqrt(0.5))
        elif 8 * step == 3 * count:
            turned = ((imag - real) * math.sqrt(0.5), (real + imag) * -math.sqrt(0.5))
        else:
            angle = -2.0 * math.pi * step / count
            cosine, sine = math.cos(angle), math.sin(angle)
            turned = (real * cosine - imag * sine, real * sine + imag * cosine)
        head.append((even[step][0] + turned[0], even[step][1] + turned[1]))
        tail.append((even[step][0] - turned[0], even[step][1] - turned[1]))
    return head + tail


def powered(first, count):
    powers = [None, first]
    for step in range(2, count):
        half = step // 2
        powers.append(times(powers[half], powers[step - half]))
    return powers


def grow(peak, scale):
    code = 0.0
    for step in STEPS:
        grown = scale * 2.0**step
        fits = peak * grown <= PEAK
        scale = jnp.where(fits, grown, scale)
        code = jnp.where(fits, code + step, code)
    return scale, code


def shrink(code, scale):
    factor = jnp.full(code.shape, scale, F32)
    for step in STEPS:
        taken = code >= step
        factor = jnp.where(taken, factor * 2.0**-step, factor)
        code = jnp.where(taken, code - step, code)
    return factor


def columns_kernel(groups, series_ref, out_ref, turned):
    rows, width = series_ref.shape
    scale, code = grow(jnp.max(jnp.abs(series_ref[...])), 1.0)
    inner = out_ref.shape[1] - 8
    for dest in range(groups):
        out_ref[dest, inner : inner + 8, :] = jnp.full((8, LANES), code, F32)
    per_row = width // groups
    tall = rows // LANES
    for high in range(tall):
        turned[...] = (series_ref[high * LANES : (high + 1) * LANES, :] * scale).T
        for dest in range(groups):
            out_ref[dest, pl.ds(high, per_row, stride=tall), :] = turned[
                pl.ds(dest, per_row, stride=groups), :
            ]


def spread_samples(series, groups):
    rows, width = series.shape
    per_row = width // groups
    inner = rows * width // (LANES * LANES)
    tall = LANES // groups
    if per_row == inner:
        return pl.pallas_call(
            lambda *refs: columns_kernel(groups, *refs),
            out_shape=jax.ShapeDtypeStruct((groups, inner * tall + 8, LANES), F32),
            in_specs=[VMEM_SPEC],
            out_specs=VMEM_SPEC,
        compiler_params=ROOM,
            scratch_shapes=[pltpu.VMEM((width, LANES), F32)],
        )(series)
    scale, code = grow(jnp.max(jnp.abs(series)), F32(1.0))
    shaped = (series * scale).reshape(tall, LANES, inner // per_row, per_row, groups)
    moving = jnp.transpose(shaped, (4, 2, 3, 0, 1)).reshape(groups, inner * tall, LANES)
    return jnp.concatenate([moving, jnp.full((groups, 8, LANES), code, F32)], axis=1)


def local_kernel(
    groups, unit, y_ref, w1_ref, w2_ref, t1_ref, t2_ref, out_ref, level_ref, rhs, lhs, mid, bins, edge
):
    inner = mid.shape[0]
    taken = y_ref.shape[1] - 8
    tall = taken // inner
    own = out_ref.shape[1] // 2 - 4
    codes = y_ref[:, taken:, :]
    least = jnp.min(codes, axis=0)
    level_ref[...] = shrink(least, unit)
    factor = shrink(codes - least[None], 1.0)
    factor = factor[:, :tall, :] if tall <= 8 else factor[:, :1, :]
    for pair in range(inner // 2):
        for part in range(2):
            step = 2 * pair + part
            block = y_ref[:, step * tall : (step + 1) * tall, :] * factor
            block = block.reshape(LANES, LANES)
            high = block.astype(BF16)
            low = (block - high.astype(F32)).astype(BF16)
            cols = slice(part * LANES, (part + 1) * LANES)
            rhs[0:LANES, cols] = high
            rhs[LANES : 2 * LANES, cols] = low
            rhs[2 * LANES : 3 * LANES, cols] = high
        first = jnp.dot(w1_ref[...], rhs[...], preferred_element_type=F32)
        for part in range(2):
            cols = slice(part * LANES, (part + 1) * LANES)
            turned = times(
                (first[:LANES, cols], first[LANES:, cols]), (t1_ref[0], t1_ref[1])
            )
            rows = slice(part * LANES, (part + 1) * LANES)
            for comp in range(2):
                high = turned[comp].astype(BF16)
                low = (turned[comp] - high.astype(F32)).astype(BF16)
                at = comp * LANES
                lhs[rows, at : at + LANES] = high
                lhs[rows, 2 * LANES + at : 3 * LANES + at] = low
                lhs[rows, 4 * LANES + at : 5 * LANES + at] = high
        second = lax.dot_general(
            w2_ref[...], lhs[...], (((1,), (1,)), ((), ())), preferred_element_type=F32
        )
        mid[2 * pair] = second[:, :LANES]
        mid[2 * pair + 1] = second[:, LANES:]

    def combine(chunk, carry):
        rows = pl.ds(pl.multiple_of(chunk * 8, 8), 8)
        rows_im = pl.ds(pl.multiple_of(LANES + chunk * 8, 8), 8)
        powers = powered((t2_ref[0, rows, :], t2_ref[1, rows, :]), inner)
        values = [(mid[0, rows, :], mid[0, rows_im, :])]
        for step in range(1, inner):
            values.append(times((mid[step, rows, :], mid[step, rows_im, :]), powers[step]))
        result = small_fft(values)
        for comp in range(2):
            for step in range(inner // 2):
                at = pl.multiple_of(8 + step * LANES + chunk * 8, 8)
                bins[comp, pl.ds(at, 8), :] = result[step][comp]
            edge[comp, rows, :] = result[inner // 2][comp]
            edge[2 + comp, rows, :] = result[inner - 1][comp]
        return carry

    lax.fori_loop(0, LANES // 8, combine, 0)
    total = inner // 2 * LANES
    for comp in range(2):
        bins[comp, 0:8, :] = edge[2 + comp, LANES - 8 : LANES, :]
        bins[comp, 8 + total : 16 + total, :] = edge[comp, 0:8, :]
    for dest in range(groups):
        base = 8 + own * dest
        for comp in range(2):
            out_ref[dest, comp * own : (comp + 1) * own, :] = bins[comp, base : base + own, :]
            at = 2 * own + 4 * comp
            out_ref[dest, at : at + 2, :] = bins[comp, base - 2 : base, :]
            out_ref[dest, at + 2 : at + 4, :] = bins[comp, base + own : base + own + 2, :]


def local_transform(moved, groups, unit, w1, w2, t1, t2):
    inner = (moved.shape[1] - 8) * groups // LANES
    total = inner // 2 * LANES
    own = total // groups
    return pl.pallas_call(
        lambda *refs: local_kernel(groups, unit, *refs),
        out_shape=(
            jax.ShapeDtypeStruct((groups, 2 * own + 8, LANES), F32),
            jax.ShapeDtypeStruct((8, LANES), F32),
        ),
        in_specs=[VMEM_SPEC] * 5,
        out_specs=(VMEM_SPEC, VMEM_SPEC),
        compiler_params=ROOM,
        scratch_shapes=[
            pltpu.VMEM((3 * LANES, 2 * LANES), BF16),
            pltpu.VMEM((2 * LANES, 6 * LANES), BF16),
            pltpu.VMEM((inner, 2 * LANES, LANES), F32),
            pltpu.VMEM((2, total + 16, LANES), F32),
            pltpu.VMEM((4, LANES, LANES), F32),
        ],
    )(moved, w1, w2, t1, t2)


def matrix_kernel(taps_ref, out_ref):
    row = lax.broadcasted_iota(jnp.int32, (LANES, LANES), 0)
    col = lax.broadcasted_iota(jnp.int32, (LANES, LANES), 1)
    below = col <= row

    def build(index, carry):
        lane = lax.broadcasted_iota(jnp.int32, (8, LANES), 1)
        source = (LANES - lane) & (LANES - 1)
        blocks = []
        for comp in range(2):
            taps = jnp.broadcast_to(taps_ref[index, pl.ds(comp, 1), :].astype(F32), (8, LANES))
            start = jnp.take_along_axis(taps, source, axis=1)
            start = jnp.broadcast_to(start[0:1, :], (LANES, LANES))
            ring = pltpu.roll(start, 0, 1, stride=1, stride_axis=0)
            blocks.append((jnp.where(below, ring, 0.0), jnp.where(below, 0.0, ring)))
        for part in range(2):
            real, imag = blocks[0][part], blocks[1][part]
            top = slice(part * LANES, (part + 1) * LANES)
            bottom = slice((2 + part) * LANES, (3 + part) * LANES)
            out_ref[index, top, 0:LANES] = real.astype(BF16)
            out_ref[index, top, LANES:] = imag.astype(BF16)
            out_ref[index, bottom, 0:LANES] = (-imag).astype(BF16)
            out_ref[index, bottom, LANES:] = real.astype(BF16)
        return carry

    lax.fori_loop(0, taps_ref.shape[0], build, 0)


def template_matrices(templates):
    count = templates.shape[0]
    return pl.pallas_call(
        matrix_kernel,
        out_shape=jax.ShapeDtypeStruct((count, 4 * LANES, 2 * LANES), BF16),
        in_specs=[VMEM_SPEC],
        out_specs=VMEM_SPEC,
        compiler_params=ROOM,
        cost_estimate=pl.CostEstimate(
            flops=count * 40 * LANES * LANES,
            bytes_accessed=count * 24 * LANES * LANES,
            transcendentals=0,
        ),
    )(templates)


def power_kernel(
    place_ref, drift_ref, z_ref, level_ref, table_ref, w_ref, out_ref, bins, rim_rows, lhs, near, far
):
    groups = z_ref.shape[0]
    own = z_ref.shape[1] // 2 - 4
    half = groups // 2
    main = groups * own
    scale = level_ref[...]

    def combine(chunk, carry):
        rows = pl.ds(pl.multiple_of(chunk * 8, 8), 8)
        rows_im = pl.ds(pl.multiple_of(own + chunk * 8, 8), 8)
        at = pl.ds(pl.multiple_of(8 + chunk * 8, 8), 8)
        powers = powered((table_ref[0, at, :], table_ref[1, at, :]), groups)
        values = [(z_ref[0, rows, :], z_ref[0, rows_im, :])]
        for step in range(1, groups):
            values.append(times((z_ref[step, rows, :], z_ref[step, rows_im, :]), powers[step]))
        result = small_fft(values)
        for step in range(groups):
            sign = level_ref[...] if step < half else -level_ref[...]
            bins[step, 0, at, :] = result[step][0] * level_ref[...]
            bins[step, 1, at, :] = result[step][1] * sign
        return carry

    lax.fori_loop(0, own // 8, combine, 0)
    rim = []
    for comp in range(2):
        rim.append(
            jnp.concatenate(
                [
                    table_ref[comp, 6:8, :],
                    table_ref[comp, 8 + own : 10 + own, :],
                    table_ref[comp, 6:8, :],
                    table_ref[comp, 8 + own : 10 + own, :],
                ]
            )
        )
    powers = powered((rim[0], rim[1]), groups)
    values = []
    for step in range(groups):
        both = z_ref[step, 2 * own : 2 * own + 8, :]
        value = (both, pltpu.roll(both, 4, 0))
        values.append(times(value, powers[step]) if step else value)
    result = small_fft(values)
    for step in range(groups):
        sign = scale if step < half else -scale
        for comp in range(2):
            value = result[step][comp] * (sign if comp else scale)
            bins[step, comp, 6:8, :] = value[0:2, :]
            bins[step, comp, 8 + own : 10 + own, :] = value[2:4, :]

    lane = lax.broadcasted_iota(jnp.int32, (8, LANES), 1)
    source = (LANES - lane) & (LANES - 1)
    rank = lax.broadcasted_iota(jnp.int32, (8, LANES), 0)
    for step in range(half, groups):
        for comp in range(2):
            for chunk in range(own // 8 + 1):
                here = bins[step, comp, 8 * chunk : 8 * chunk + 8, :]
                after = bins[step, comp, 8 * chunk + 1 : 8 * chunk + 9, :]
                value = jnp.where(lane == 0, after, jnp.take_along_axis(here, source, axis=1))
                if step == half and chunk == 0:
                    value = jnp.where(place_ref[0] == 0, 0.0, value)
                bins[step, comp, 8 * chunk : 8 * chunk + 8, :] = value
    for step in range(groups):
        for comp in range(2):
            for shift in range(2):
                at = 8 + shift if step < half else 8 - shift
                cols = slice((2 * comp + shift) * LANES, (2 * comp + shift + 1) * LANES)
                lhs[step * own : (step + 1) * own, cols] = bins[
                    step, comp, at : at + own, :
                ].astype(BF16)
                at = 8 + own + shift if step < half else 7 - shift
                rim_rows[2 * comp + shift, step : step + 1, :] = bins[step, comp, at : at + 1, :]
    for part in range(4):
        lhs[main:, part * LANES : (part + 1) * LANES] = rim_rows[part].astype(BF16)

    near[...] = jnp.zeros_like(near)
    far[...] = jnp.zeros_like(far)
    pieces = max(1, main // 512)
    edges = [main // pieces * piece for piece in range(pieces)] + [main + groups]

    def template(index, carry):
        shift = drift_ref[index]
        for piece in range(pieces):
            rows = slice(edges[piece], edges[piece + 1])
            response = jnp.dot(lhs[rows, :], w_ref[index], preferred_element_type=F32)
            power = response[:, :LANES] * response[:, :LANES]
            power = power + response[:, LANES:] * response[:, LANES:]
            rolled = pltpu.roll(power, (LANES - shift) & (LANES - 1), 1)
            inside = lax.broadcasted_iota(jnp.int32, rolled.shape, 1) < LANES - shift
            near[rows, :] += jnp.where(inside, rolled, 0.0)
            far[rows, :] += jnp.where(inside, 0.0, rolled)
        return carry

    lax.fori_loop(0, w_ref.shape[0], template, 0)
    peak = jnp.zeros((8, LANES), F32)
    for step in range(groups):
        base = step * own
        spare = far[main + step : main + step + 1, :]
        if step < half:
            dest = 2 * step
            out_ref[dest, 0:own, :] = near[base : base + own, :] + far[base + 1 : base + own + 1, :]
            out_ref[dest, own - 1 : own, :] = near[base + own - 1 : base + own, :] + spare
        else:
            dest = 2 * (groups - 1 - step) + 1
            out_ref[dest, 0:own, :] = near[base : base + own, :] + far[base - 1 : base + own - 1, :]
            out_ref[dest, 0:1, :] = near[base : base + 1, :] + spare
        for chunk in range(own // 8):
            peak = jnp.maximum(peak, out_ref[dest, 8 * chunk : 8 * chunk + 8, :])
    scale, code = grow(jnp.max(peak), REACH)
    for dest in range(groups):
        out_ref[dest, 0:own, :] = out_ref[dest, 0:own, :] * scale
        out_ref[dest, own : own + 8, :] = jnp.full((8, LANES), code, F32)


def template_powers(place, drift, moved, level, table, matrices):
    groups = moved.shape[0]
    own = moved.shape[1] // 2 - 4
    rows = groups * own + groups
    return pl.pallas_call(
        power_kernel,
        out_shape=jax.ShapeDtypeStruct((groups, own + 8, LANES), F32),
        in_specs=[SMEM_SPEC, SMEM_SPEC] + [VMEM_SPEC] * 4,
        out_specs=VMEM_SPEC,
        compiler_params=ROOM,
        scratch_shapes=[
            pltpu.VMEM((groups, 2, own + 24, LANES), F32),
            pltpu.VMEM((4, groups, LANES), F32),
            pltpu.VMEM((rows, 4 * LANES), BF16),
            pltpu.VMEM((rows, LANES), F32),
            pltpu.VMEM((rows, LANES), F32),
        ],
    )(place, drift, moved, level, table, matrices)


def place_kernel(place_ref, power_ref, out_ref):
    groups, own = power_ref.shape[0], power_ref.shape[1] - 8
    total = groups * own
    flip = 7 - lax.broadcasted_iota(jnp.int32, (8, LANES), 0)

    @pl.when(place_ref[0] % 2 == 0)
    def _():
        for source in range(groups):
            factor = shrink(power_ref[source, own:, :], 1.0 / REACH)
            for chunk in range(own // 8):
                at = source * own + 8 * chunk
                value = power_ref[source, 8 * chunk : 8 * chunk + 8, :] * factor
                out_ref[at : at + 8, :] = value

    @pl.when(place_ref[0] % 2 == 1)
    def _():
        for source in range(groups):
            factor = shrink(power_ref[source, own:, :], 1.0 / REACH)
            for chunk in range(own // 8):
                at = total - source * own - 8 * chunk - 8
                value = power_ref[source, 8 * chunk : 8 * chunk + 8, :] * factor
                out_ref[at : at + 8, :] = jnp.take_along_axis(value, flip, axis=0)


def place_powers(place, moved):
    groups, own = moved.shape[0], moved.shape[1] - 8
    return pl.pallas_call(
        place_kernel,
        out_shape=jax.ShapeDtypeStruct((groups * own, LANES), F32),
        in_specs=[SMEM_SPEC, VMEM_SPEC],
        out_specs=VMEM_SPEC,
        compiler_params=ROOM,
    )(place, moved)


def exchange(value):
    moved = lax.all_to_all(value.astype(F16), AXES, split_axis=0, concat_axis=0, tiled=True)
    return moved.astype(F32)


def body(series, templates, drift):
    groups = lax.axis_size(AXES)
    place = lax.axis_index(AXES)
    samples = series.shape[0] * series.shape[1]
    length = samples * groups
    inner = samples // (LANES * LANES)
    total = inner // 2 * LANES
    own = total // groups
    index = np.arange(LANES, dtype=np.int64)
    w1 = jnp.asarray(first_matrix())
    w2 = jnp.asarray(second_matrix(2.0 / samples))
    t1 = jnp.asarray(table_pair(index[:, None] * index[None, :], LANES * LANES))
    t2 = jnp.asarray(table_pair(LANES * index[:, None] + index[None, :], samples))
    rows = np.arange(-8, total + 8, dtype=np.int64)
    wide = jnp.asarray(table_pair(LANES * rows[:, None] + index[None, :], length))
    table = lax.dynamic_slice_in_dim(wide, place * own, own + 16, axis=1)
    place = place.astype(jnp.int32).reshape(1)

    matrices = template_matrices(templates)
    moved = exchange(spread_samples(series, groups))
    unit = samples / 2 / math.sqrt(length)
    partial, level = local_transform(moved, groups, unit, w1, w2, t1, t2)
    moved = exchange(partial)
    power = template_powers(place, drift, moved, level, table, matrices)
    return place_powers(place, exchange(power))


def solution(mesh):
    in_specs = (P(("band", "gx", "gy"), None), P(), P())
    out_specs = P(("band", "gx", "gy"), None)
    return jax.shard_map(body, mesh=mesh, in_specs=in_specs, out_specs=out_specs, check_vma=False)
```

```python
import math

import jax
import jax.numpy as jnp
import numpy as np
from jax import lax
from jax.experimental import pallas as pl
from jax.experimental.pallas import tpu as pltpu
from jax.sharding import PartitionSpec as P

LANES = 128
AXES = ("gx", "gy")
VMEM_SPEC = pl.BlockSpec(memory_space=pltpu.VMEM)
SMEM_SPEC = pl.BlockSpec(memory_space=pltpu.SMEM)
F32 = jnp.float32
F16 = jnp.float16
STEPS = (64, 32, 16, 8, 4, 2, 1)
PEAK = 2.0**14
REACH = 2.0**-40
ROOM = pltpu.CompilerParams(vmem_limit_bytes=20 * 2**20)
WIDE = pltpu.CompilerParams(vmem_limit_bytes=50 * 2**20)
BF16 = jnp.bfloat16


def split_pair(table):
    high = np.asarray(table, np.float32).astype(BF16)
    low = (np.asarray(table, np.float64) - high.astype(np.float64)).astype(BF16)
    return high, low


def phases(product, length):
    angle = (product % length).astype(np.float64) * (-2.0 * np.pi / length)
    return np.cos(angle), np.sin(angle)


def first_matrix():
    index = np.arange(LANES, dtype=np.int64)
    real, imag = phases(index[:, None] * index[None, :], LANES)
    high, low = split_pair(np.concatenate([real, imag], axis=0))
    return np.concatenate([high, high, low], axis=1)


def second_matrix(gain):
    index = np.arange(LANES, dtype=np.int64)
    real, imag = phases(index[:, None] * index[None, :], LANES)
    real, imag = real * gain, imag * gain
    top = np.concatenate([real, -imag], axis=1)
    bottom = np.concatenate([imag, real], axis=1)
    high, low = split_pair(np.concatenate([top, bottom], axis=0))
    return np.concatenate([high, high, low], axis=1)


def table_pair(product, length):
    return np.stack(phases(product, length)).astype(np.float32)


def times(left, right):
    return (
        left[0] * right[0] - left[1] * right[1],
        left[0] * right[1] + left[1] * right[0],
    )


def small_fft(values):
    count = len(values)
    if count == 1:
        return values
    even = small_fft(values[0::2])
    odd = small_fft(values[1::2])
    head, tail = [], []
    for step in range(count // 2):
        real, imag = odd[step]
        if step == 0:
            turned = (real, imag)
        elif 4 * step == count:
            turned = (imag, -real)
        elif 8 * step == count:
            turned = ((real + imag) * math.sqrt(0.5), (imag - real) * math.sqrt(0.5))
        elif 8 * step == 3 * count:
            turned = ((imag - real) * math.sqrt(0.5), (real + imag) * -math.sqrt(0.5))
        else:
            angle = -2.0 * math.pi * step / count
            cosine, sine = math.cos(angle), math.sin(angle)
            turned = (real * cosine - imag * sine, real * sine + imag * cosine)
        head.append((even[step][0] + turned[0], even[step][1] + turned[1]))
        tail.append((even[step][0] - turned[0], even[step][1] - turned[1]))
    return head + tail


def powered(first, count):
    powers = [None, first]
    for step in range(2, count):
        half = step // 2
        powers.append(times(powers[half], powers[step - half]))
    return powers


def grow(peak, scale):
    code = 0.0
    for step in STEPS:
        grown = scale * 2.0**step
        fits = peak * grown <= PEAK
        scale = jnp.where(fits, grown, scale)
        code = jnp.where(fits, code + step, code)
    return scale, code


def shrink(code, scale):
    factor = jnp.full(code.shape, scale, F32)
    for step in STEPS:
        taken = code >= step
        factor = jnp.where(taken, factor * 2.0**-step, factor)
        code = jnp.where(taken, code - step, code)
    return factor


def columns_kernel(groups, series_ref, out_ref, turned):
    rows, width = series_ref.shape
    scale, code = grow(jnp.max(jnp.abs(series_ref[...])), 1.0)
    inner = out_ref.shape[1] - 8
    for dest in range(groups):
        out_ref[dest, inner : inner + 8, :] = jnp.full((8, LANES), code, F32)
    per_row = width // groups
    tall = rows // LANES
    for high in range(tall):
        turned[...] = (series_ref[high * LANES : (high + 1) * LANES, :] * scale).T
        for dest in range(groups):
            out_ref[dest, pl.ds(high, per_row, stride=tall), :] = turned[
                pl.ds(dest, per_row, stride=groups), :
            ]


def spread_samples(series, groups):
    rows, width = series.shape
    per_row = width // groups
    inner = rows * width // (LANES * LANES)
    tall = LANES // groups
    if per_row == inner:
        return pl.pallas_call(
            lambda *refs: columns_kernel(groups, *refs),
            out_shape=jax.ShapeDtypeStruct((groups, inner * tall + 8, LANES), F32),
            in_specs=[VMEM_SPEC],
            out_specs=VMEM_SPEC,
            compiler_params=ROOM,
            scratch_shapes=[pltpu.VMEM((width, LANES), F32)],
        )(series)
    scale, code = grow(jnp.max(jnp.abs(series)), F32(1.0))
    shaped = (series * scale).reshape(tall, LANES, inner // per_row, per_row, groups)
    moving = jnp.transpose(shaped, (4, 2, 3, 0, 1)).reshape(groups, inner * tall, LANES)
    return jnp.concatenate([moving, jnp.full((groups, 8, LANES), code, F32)], axis=1)


def local_kernel(
    groups,
    unit,
    y_ref,
    w1_ref,
    w2_ref,
    t1_ref,
    t2_ref,
    out_ref,
    level_ref,
    rhs,
    lhs,
    mid,
    bins,
    edge,
):
    inner = mid.shape[0]
    taken = y_ref.shape[1] - 8
    tall = taken // inner
    own = out_ref.shape[1] // 2 - 4
    codes = y_ref[:, taken:, :]
    least = jnp.min(jnp.min(codes, axis=0), axis=0, keepdims=True)
    least = jnp.broadcast_to(least, level_ref.shape)
    level_ref[...] = shrink(least, unit)
    factor = shrink(codes - least[None], 1.0)
    factor = factor[:, :tall, :] if tall <= 8 else factor[:, :1, :]
    for pair in range(inner // 2):
        for part in range(2):
            step = 2 * pair + part
            block = y_ref[:, step * tall : (step + 1) * tall, :] * factor
            block = block.reshape(LANES, LANES)
            high = block.astype(BF16)
            low = (block - high.astype(F32)).astype(BF16)
            cols = slice(part * LANES, (part + 1) * LANES)
            rhs[0:LANES, cols] = high
            rhs[LANES : 2 * LANES, cols] = low
            rhs[2 * LANES : 3 * LANES, cols] = high
        first = jnp.dot(w1_ref[...], rhs[...], preferred_element_type=F32)
        for part in range(2):
            cols = slice(part * LANES, (part + 1) * LANES)
            turned = times(
                (first[:LANES, cols], first[LANES:, cols]), (t1_ref[0], t1_ref[1])
            )
            rows = slice(part * LANES, (part + 1) * LANES)
            for comp in range(2):
                high = turned[comp].astype(BF16)
                low = (turned[comp] - high.astype(F32)).astype(BF16)
                at = comp * LANES
                lhs[rows, at : at + LANES] = high
                lhs[rows, 2 * LANES + at : 3 * LANES + at] = low
                lhs[rows, 4 * LANES + at : 5 * LANES + at] = high
        second = lax.dot_general(
            w2_ref[...], lhs[...], (((1,), (1,)), ((), ())), preferred_element_type=F32
        )
        mid[2 * pair] = second[:, :LANES]
        mid[2 * pair + 1] = second[:, LANES:]

    def combine(chunk, carry):
        rows = pl.ds(pl.multiple_of(chunk * 8, 8), 8)
        rows_im = pl.ds(pl.multiple_of(LANES + chunk * 8, 8), 8)
        powers = powered((t2_ref[0, rows, :], t2_ref[1, rows, :]), inner)
        values = [(mid[0, rows, :], mid[0, rows_im, :])]
        for step in range(1, inner):
            values.append(times((mid[step, rows, :], mid[step, rows_im, :]), powers[step]))
        result = small_fft(values)
        for comp in range(2):
            for step in range(inner // 2):
                at = pl.multiple_of(8 + step * LANES + chunk * 8, 8)
                bins[comp, pl.ds(at, 8), :] = result[step][comp]
            edge[comp, rows, :] = result[inner // 2][comp]
            edge[2 + comp, rows, :] = result[inner - 1][comp]
        return carry

    lax.fori_loop(0, LANES // 8, combine, 0)
    total = inner // 2 * LANES
    for comp in range(2):
        bins[comp, 0:8, :] = edge[2 + comp, LANES - 8 : LANES, :]
        bins[comp, 8 + total : 16 + total, :] = edge[comp, 0:8, :]
    for dest in range(groups):
        base = 8 + own * dest
        for comp in range(2):
            out_ref[dest, comp * own : (comp + 1) * own, :] = bins[comp, base : base + own, :]
            at = 2 * own + 4 * comp
            out_ref[dest, at : at + 2, :] = bins[comp, base - 2 : base, :]
            out_ref[dest, at + 2 : at + 4, :] = bins[comp, base + own : base + own + 2, :]


def local_transform(moved, groups, unit, w1, w2, t1, t2):
    inner = (moved.shape[1] - 8) * groups // LANES
    total = inner // 2 * LANES
    own = total // groups
    return pl.pallas_call(
        lambda *refs: local_kernel(groups, unit, *refs),
        out_shape=(
            jax.ShapeDtypeStruct((groups, 2 * own + 8, LANES), F32),
            jax.ShapeDtypeStruct((8, LANES), F32),
        ),
        in_specs=[VMEM_SPEC] * 5,
        out_specs=(VMEM_SPEC, VMEM_SPEC),
        compiler_params=ROOM,
        scratch_shapes=[
            pltpu.VMEM((3 * LANES, 2 * LANES), BF16),
            pltpu.VMEM((2 * LANES, 6 * LANES), BF16),
            pltpu.VMEM((inner, 2 * LANES, LANES), F32),
            pltpu.VMEM((2, total + 16, LANES), F32),
            pltpu.VMEM((4, LANES, LANES), F32),
        ],
    )(moved, w1, w2, t1, t2)


def matrix_kernel(taps_ref, stored_ref, out_ref, sent):
    row = lax.broadcasted_iota(jnp.int32, (LANES, LANES), 0)
    col = lax.broadcasted_iota(jnp.int32, (LANES, LANES), 1)
    below = col <= row

    def build(index, carry):
        lane = lax.broadcasted_iota(jnp.int32, (8, LANES), 1)
        source = (LANES - lane) & (LANES - 1)
        blocks = []
        for comp in range(2):
            taps = jnp.broadcast_to(taps_ref[index, pl.ds(comp, 1), :].astype(F32), (8, LANES))
            start = jnp.take_along_axis(taps, source, axis=1)
            start = jnp.broadcast_to(start[0:1, :], (LANES, LANES))
            ring = pltpu.roll(start, 0, 1, stride=1, stride_axis=0)
            blocks.append((jnp.where(below, ring, 0.0), jnp.where(below, 0.0, ring)))
        for part in range(2):
            real, imag = blocks[0][part], blocks[1][part]
            top = slice(part * LANES, (part + 1) * LANES)
            bottom = slice((2 + part) * LANES, (3 + part) * LANES)
            out_ref[index, top, 0:LANES] = real.astype(BF16)
            out_ref[index, top, LANES:] = imag.astype(BF16)
            out_ref[index, bottom, 0:LANES] = (-imag).astype(BF16)
            out_ref[index, bottom, LANES:] = real.astype(BF16)
        return carry

    lax.fori_loop(0, taps_ref.shape[0], build, 0)
    copy = pltpu.make_async_copy(out_ref, stored_ref.at[pl.ds(0, out_ref.shape[0])], sent)
    copy.start()
    copy.wait()


def template_matrices(templates):
    count = templates.shape[0]
    return pl.pallas_call(
        matrix_kernel,
        out_shape=jax.ShapeDtypeStruct((4 * count, 4 * LANES, 2 * LANES), BF16),
        in_specs=[VMEM_SPEC],
        out_specs=pl.BlockSpec(memory_space=pl.ANY),
        scratch_shapes=[
            pltpu.VMEM((count, 4 * LANES, 2 * LANES), BF16),
            pltpu.SemaphoreType.DMA,
        ],
        compiler_params=WIDE,
        cost_estimate=pl.CostEstimate(
            flops=count * 40 * LANES * LANES,
            bytes_accessed=count * 24 * LANES * LANES,
            transcendentals=0,
        ),
    )(templates)


def power_kernel(
    place_ref,
    drift_ref,
    z_ref,
    level_ref,
    table_ref,
    matrices_ref,
    out_ref,
    bins,
    rim_rows,
    lhs,
    near,
    far,
    w_ref,
    arrived,
):
    fetch = pltpu.make_async_copy(matrices_ref.at[pl.ds(0, w_ref.shape[0])], w_ref, arrived)
    fetch.start()
    groups = z_ref.shape[0]
    own = z_ref.shape[1] // 2 - 4
    half = groups // 2
    main = groups * own
    scale = level_ref[...]

    def combine(chunk, carry):
        rows = pl.ds(pl.multiple_of(chunk * 8, 8), 8)
        rows_im = pl.ds(pl.multiple_of(own + chunk * 8, 8), 8)
        at = pl.ds(pl.multiple_of(8 + chunk * 8, 8), 8)
        powers = powered((table_ref[0, at, :], table_ref[1, at, :]), groups)
        values = [(z_ref[0, rows, :], z_ref[0, rows_im, :])]
        for step in range(1, groups):
            values.append(times((z_ref[step, rows, :], z_ref[step, rows_im, :]), powers[step]))
        result = small_fft(values)
        for step in range(groups):
            sign = level_ref[...] if step < half else -level_ref[...]
            bins[step, 0, at, :] = result[step][0] * level_ref[...]
            bins[step, 1, at, :] = result[step][1] * sign
        return carry

    lax.fori_loop(0, own // 8, combine, 0)
    rim = []
    for comp in range(2):
        rim.append(
            jnp.concatenate(
                [
                    table_ref[comp, 6:8, :],
                    table_ref[comp, 8 + own : 10 + own, :],
                    table_ref[comp, 6:8, :],
                    table_ref[comp, 8 + own : 10 + own, :],
                ]
            )
        )
    powers = powered((rim[0], rim[1]), groups)
    values = []
    for step in range(groups):
        both = z_ref[step, 2 * own : 2 * own + 8, :]
        value = (both, pltpu.roll(both, 4, 0))
        values.append(times(value, powers[step]) if step else value)
    result = small_fft(values)
    for step in range(groups):
        sign = scale if step < half else -scale
        for comp in range(2):
            value = result[step][comp] * (sign if comp else scale)
            bins[step, comp, 6:8, :] = value[0:2, :]
            bins[step, comp, 8 + own : 10 + own, :] = value[2:4, :]

    lane = lax.broadcasted_iota(jnp.int32, (8, LANES), 1)
    source = (LANES - lane) & (LANES - 1)
    rank = lax.broadcasted_iota(jnp.int32, (8, LANES), 0)
    for step in range(half, groups):
        for comp in range(2):
            for chunk in range(own // 8 + 1):
                here = bins[step, comp, 8 * chunk : 8 * chunk + 8, :]
                after = bins[step, comp, 8 * chunk + 1 : 8 * chunk + 9, :]
                value = jnp.where(lane == 0, after, jnp.take_along_axis(here, source, axis=1))
                if step == half and chunk == 0:
                    value = jnp.where(place_ref[0] == 0, 0.0, value)
                bins[step, comp, 8 * chunk : 8 * chunk + 8, :] = value
    for step in range(groups):
        for comp in range(2):
            for shift in range(2):
                at = 8 + shift if step < half else 8 - shift
                cols = slice((2 * comp + shift) * LANES, (2 * comp + shift + 1) * LANES)
                lhs[step * own : (step + 1) * own, cols] = bins[
                    step, comp, at : at + own, :
                ].astype(BF16)
                at = 8 + own + shift if step < half else 7 - shift
                rim_rows[2 * comp + shift, step : step + 1, :] = bins[step, comp, at : at + 1, :]
    for part in range(4):
        lhs[main:, part * LANES : (part + 1) * LANES] = rim_rows[part].astype(BF16)

    near[...] = jnp.zeros_like(near)
    far[...] = jnp.zeros_like(far)
    pieces = max(1, main // 512)
    edges = [main // pieces * piece for piece in range(pieces)] + [main + groups]

    fetch.wait()
    count = w_ref.shape[0]
    batch = math.gcd(count, 8)

    def template(turn, carry):
        for piece in range(pieces):
            rows = slice(edges[piece], edges[piece + 1])
            here, past = None, None
            for member in range(batch):
                index = turn * batch + member
                shift = drift_ref[index]
                response = jnp.dot(lhs[rows, :], w_ref[index], preferred_element_type=F32)
                power = response[:, :LANES] * response[:, :LANES]
                power = power + response[:, LANES:] * response[:, LANES:]
                rolled = pltpu.roll(power, (LANES - shift) & (LANES - 1), 1)
                inside = lax.broadcasted_iota(jnp.int32, rolled.shape, 1) < LANES - shift
                kept, moved = jnp.where(inside, rolled, 0.0), jnp.where(inside, 0.0, rolled)
                here = kept if here is None else here + kept
                past = moved if past is None else past + moved
            near[rows, :] += here
            far[rows, :] += past
        return carry

    lax.fori_loop(0, count // batch, template, 0)
    peak = jnp.zeros((8, LANES), F32)
    for step in range(groups):
        base = step * own
        spare = far[main + step : main + step + 1, :]
        if step < half:
            dest = 2 * step
            out_ref[dest, 0:own, :] = near[base : base + own, :] + far[base + 1 : base + own + 1, :]
            out_ref[dest, own - 1 : own, :] = near[base + own - 1 : base + own, :] + spare
        else:
            dest = 2 * (groups - 1 - step) + 1
            out_ref[dest, 0:own, :] = near[base : base + own, :] + far[base - 1 : base + own - 1, :]
            out_ref[dest, 0:1, :] = near[base : base + 1, :] + spare
        for chunk in range(own // 8):
            peak = jnp.maximum(peak, out_ref[dest, 8 * chunk : 8 * chunk + 8, :])
    scale, code = grow(jnp.max(peak), REACH)
    for dest in range(groups):
        out_ref[dest, 0:own, :] = out_ref[dest, 0:own, :] * scale
        out_ref[dest, own : own + 8, :] = jnp.full((8, LANES), code, F32)


def template_powers(place, drift, moved, level, table, matrices):
    groups = moved.shape[0]
    own = moved.shape[1] // 2 - 4
    rows = groups * own + groups
    return pl.pallas_call(
        power_kernel,
        out_shape=jax.ShapeDtypeStruct((groups, own + 8, LANES), F32),
        in_specs=[SMEM_SPEC, SMEM_SPEC] + [VMEM_SPEC] * 3 + [pl.BlockSpec(memory_space=pl.ANY)],
        out_specs=VMEM_SPEC,
        compiler_params=WIDE,
        scratch_shapes=[
            pltpu.VMEM((groups, 2, own + 24, LANES), F32),
            pltpu.VMEM((4, groups, LANES), F32),
            pltpu.VMEM((rows, 4 * LANES), BF16),
            pltpu.VMEM((rows, LANES), F32),
            pltpu.VMEM((rows, LANES), F32),
            pltpu.VMEM((drift.shape[0], 4 * LANES, 2 * LANES), BF16),
            pltpu.SemaphoreType.DMA,
        ],
    )(place, drift, moved, level, table, matrices)


def place_kernel(place_ref, power_ref, out_ref):
    groups, own = power_ref.shape[0], power_ref.shape[1] - 8
    total = groups * own
    flip = 7 - lax.broadcasted_iota(jnp.int32, (8, LANES), 0)

    @pl.when(place_ref[0] % 2 == 0)
    def _():
        for source in range(groups):
            factor = shrink(power_ref[source, own:, :], 1.0 / REACH)
            for chunk in range(own // 8):
                at = source * own + 8 * chunk
                value = power_ref[source, 8 * chunk : 8 * chunk + 8, :] * factor
                out_ref[at : at + 8, :] = value

    @pl.when(place_ref[0] % 2 == 1)
    def _():
        for source in range(groups):
            factor = shrink(power_ref[source, own:, :], 1.0 / REACH)
            for chunk in range(own // 8):
                at = total - source * own - 8 * chunk - 8
                value = power_ref[source, 8 * chunk : 8 * chunk + 8, :] * factor
                out_ref[at : at + 8, :] = jnp.take_along_axis(value, flip, axis=0)


def place_powers(place, moved):
    groups, own = moved.shape[0], moved.shape[1] - 8
    return pl.pallas_call(
        place_kernel,
        out_shape=jax.ShapeDtypeStruct((groups * own, LANES), F32),
        in_specs=[SMEM_SPEC, VMEM_SPEC],
        out_specs=VMEM_SPEC,
        compiler_params=ROOM,
    )(place, moved)


def exchange(value):
    moved = lax.all_to_all(value.astype(F16), AXES, split_axis=0, concat_axis=0, tiled=True)
    return moved.astype(F32)


def body(series, templates, drift):
    groups = lax.axis_size(AXES)
    place = lax.axis_index(AXES)
    samples = series.shape[0] * series.shape[1]
    length = samples * groups
    inner = samples // (LANES * LANES)
    total = inner // 2 * LANES
    own = total // groups
    index = np.arange(LANES, dtype=np.int64)
    w1 = jnp.asarray(first_matrix())
    w2 = jnp.asarray(second_matrix(2.0 / samples))
    t1 = jnp.asarray(table_pair(index[:, None] * index[None, :], LANES * LANES))
    t2 = jnp.asarray(table_pair(LANES * index[:, None] + index[None, :], samples))
    rows = np.arange(-8, total + 8, dtype=np.int64)
    wide = jnp.asarray(table_pair(LANES * rows[:, None] + index[None, :], length))
    table = lax.dynamic_slice_in_dim(wide, place * own, own + 16, axis=1)
    place = place.astype(jnp.int32).reshape(1)

    matrices = template_matrices(templates)
    moved = exchange(spread_samples(series, groups))
    unit = samples / 2 / math.sqrt(length)
    partial, level = local_transform(moved, groups, unit, w1, w2, t1, t2)
    moved = exchange(partial)
    power = template_powers(place, drift, moved, level, table, matrices)
    return place_powers(place, exchange(power))


def solution(mesh):
    in_specs = (P(("band", "gx", "gy"), None), P(), P())
    out_specs = P(("band", "gx", "gy"), None)
    return jax.shard_map(body, mesh=mesh, in_specs=in_specs, out_specs=out_specs, check_vma=False)
```

```python
import math

import jax
import jax.numpy as jnp
import numpy as np
from jax import lax
from jax.experimental import pallas as pl
from jax.experimental.pallas import tpu as pltpu
from jax.sharding import PartitionSpec as P

LANES = 128
AXES = ("gx", "gy")
VMEM_SPEC = pl.BlockSpec(memory_space=pltpu.VMEM)
SMEM_SPEC = pl.BlockSpec(memory_space=pltpu.SMEM)
F32 = jnp.float32
F16 = jnp.float16
STEPS = (64, 32, 16, 8, 4, 2, 1)
PEAK = 2.0**14
REACH = 2.0**-40
ROOM = pltpu.CompilerParams(vmem_limit_bytes=20 * 2**20)
WIDE = pltpu.CompilerParams(vmem_limit_bytes=50 * 2**20)
BF16 = jnp.bfloat16


def split_pair(table):
    high = np.asarray(table, np.float32).astype(BF16)
    low = (np.asarray(table, np.float64) - high.astype(np.float64)).astype(BF16)
    return high, low


def phases(product, length):
    angle = (product % length).astype(np.float64) * (-2.0 * np.pi / length)
    return np.cos(angle), np.sin(angle)


def first_matrix():
    index = np.arange(LANES, dtype=np.int64)
    real, imag = phases(index[:, None] * index[None, :], LANES)
    high, low = split_pair(np.concatenate([real, imag], axis=0))
    return np.concatenate([high, high, low], axis=1)


def second_matrix(gain):
    index = np.arange(LANES, dtype=np.int64)
    real, imag = phases(index[:, None] * index[None, :], LANES)
    real, imag = real * gain, imag * gain
    top = np.concatenate([real, -imag], axis=1)
    bottom = np.concatenate([imag, real], axis=1)
    high, low = split_pair(np.concatenate([top, bottom], axis=0))
    return np.concatenate([high, high, low], axis=1)


def table_pair(product, length):
    return np.stack(phases(product, length)).astype(np.float32)


def times(left, right):
    return (
        left[0] * right[0] - left[1] * right[1],
        left[0] * right[1] + left[1] * right[0],
    )


def small_fft(values):
    count = len(values)
    if count == 1:
        return values
    even = small_fft(values[0::2])
    odd = small_fft(values[1::2])
    head, tail = [], []
    for step in range(count // 2):
        real, imag = odd[step]
        if step == 0:
            turned = (real, imag)
        elif 4 * step == count:
            turned = (imag, -real)
        elif 8 * step == count:
            turned = ((real + imag) * math.sqrt(0.5), (imag - real) * math.sqrt(0.5))
        elif 8 * step == 3 * count:
            turned = ((imag - real) * math.sqrt(0.5), (real + imag) * -math.sqrt(0.5))
        else:
            angle = -2.0 * math.pi * step / count
            cosine, sine = math.cos(angle), math.sin(angle)
            turned = (real * cosine - imag * sine, real * sine + imag * cosine)
        head.append((even[step][0] + turned[0], even[step][1] + turned[1]))
        tail.append((even[step][0] - turned[0], even[step][1] - turned[1]))
    return head + tail


def powered(first, count):
    powers = [None, first]
    for step in range(2, count):
        half = step // 2
        powers.append(times(powers[half], powers[step - half]))
    return powers


def grow(peak, scale):
    code = 0.0
    for step in STEPS:
        grown = scale * 2.0**step
        fits = peak * grown <= PEAK
        scale = jnp.where(fits, grown, scale)
        code = jnp.where(fits, code + step, code)
    return scale, code


def shrink(code, scale):
    factor = jnp.full(code.shape, scale, F32)
    for step in STEPS:
        taken = code >= step
        factor = jnp.where(taken, factor * 2.0**-step, factor)
        code = jnp.where(taken, code - step, code)
    return factor


def columns_kernel(groups, series_ref, out_ref, turned):
    rows, width = series_ref.shape
    scale, code = grow(jnp.max(jnp.abs(series_ref[...])), 1.0)
    inner = out_ref.shape[1] - 8
    for dest in range(groups):
        out_ref[dest, inner : inner + 8, :] = jnp.full((8, LANES), code, F32)
    per_row = width // groups
    tall = rows // LANES
    for high in range(tall):
        turned[...] = (series_ref[high * LANES : (high + 1) * LANES, :] * scale).T
        for dest in range(groups):
            out_ref[dest, pl.ds(high, per_row, stride=tall), :] = turned[
                pl.ds(dest, per_row, stride=groups), :
            ]


def spread_samples(series, groups):
    rows, width = series.shape
    per_row = width // groups
    inner = rows * width // (LANES * LANES)
    tall = LANES // groups
    if per_row == inner:
        return pl.pallas_call(
            lambda *refs: columns_kernel(groups, *refs),
            out_shape=jax.ShapeDtypeStruct((groups, inner * tall + 8, LANES), F32),
            in_specs=[VMEM_SPEC],
            out_specs=VMEM_SPEC,
            compiler_params=ROOM,
            scratch_shapes=[pltpu.VMEM((width, LANES), F32)],
        )(series)
    scale, code = grow(jnp.max(jnp.abs(series)), F32(1.0))
    shaped = (series * scale).reshape(tall, LANES, inner // per_row, per_row, groups)
    moving = jnp.transpose(shaped, (4, 2, 3, 0, 1)).reshape(groups, inner * tall, LANES)
    return jnp.concatenate([moving, jnp.full((groups, 8, LANES), code, F32)], axis=1)


def local_kernel(
    groups,
    unit,
    y_ref,
    w1_ref,
    w2_ref,
    t1_ref,
    t2_ref,
    out_ref,
    level_ref,
    rhs,
    lhs,
    mid,
    bins,
    edge,
):
    inner = mid.shape[0]
    taken = y_ref.shape[1] - 8
    tall = taken // inner
    own = out_ref.shape[1] // 2 - 4
    codes = y_ref[:, taken:, :]
    least = jnp.min(jnp.min(codes, axis=0), axis=0, keepdims=True)
    least = jnp.broadcast_to(least, level_ref.shape)
    level_ref[...] = shrink(least, unit)
    factor = shrink(codes - least[None], 1.0)
    factor = factor[:, :tall, :] if tall <= 8 else factor[:, :1, :]
    for pair in range(inner // 2):
        for part in range(2):
            step = 2 * pair + part
            block = y_ref[:, step * tall : (step + 1) * tall, :] * factor
            block = block.reshape(LANES, LANES)
            high = block.astype(BF16)
            low = (block - high.astype(F32)).astype(BF16)
            cols = slice(part * LANES, (part + 1) * LANES)
            rhs[pair, 0:LANES, cols] = high
            rhs[pair, LANES : 2 * LANES, cols] = low
            rhs[pair, 2 * LANES : 3 * LANES, cols] = high
    for pair in range(inner // 2):
        first = jnp.dot(w1_ref[...], rhs[pair], preferred_element_type=F32)
        for part in range(2):
            cols = slice(part * LANES, (part + 1) * LANES)
            turned = times(
                (first[:LANES, cols], first[LANES:, cols]), (t1_ref[0], t1_ref[1])
            )
            rows = slice(part * LANES, (part + 1) * LANES)
            for comp in range(2):
                high = turned[comp].astype(BF16)
                low = (turned[comp] - high.astype(F32)).astype(BF16)
                at = comp * LANES
                lhs[pair, rows, at : at + LANES] = high
                lhs[pair, rows, 2 * LANES + at : 3 * LANES + at] = low
                lhs[pair, rows, 4 * LANES + at : 5 * LANES + at] = high
    for pair in range(inner // 2):
        second = lax.dot_general(
            w2_ref[...], lhs[pair], (((1,), (1,)), ((), ())), preferred_element_type=F32
        )
        mid[2 * pair] = second[:, :LANES]
        mid[2 * pair + 1] = second[:, LANES:]

    def combine(chunk, carry):
        rows = pl.ds(pl.multiple_of(chunk * 8, 8), 8)
        rows_im = pl.ds(pl.multiple_of(LANES + chunk * 8, 8), 8)
        powers = powered((t2_ref[0, rows, :], t2_ref[1, rows, :]), inner)
        values = [(mid[0, rows, :], mid[0, rows_im, :])]
        for step in range(1, inner):
            values.append(times((mid[step, rows, :], mid[step, rows_im, :]), powers[step]))
        result = small_fft(values)
        for comp in range(2):
            for step in range(inner // 2):
                at = pl.multiple_of(8 + step * LANES + chunk * 8, 8)
                bins[comp, pl.ds(at, 8), :] = result[step][comp]
            edge[comp, rows, :] = result[inner // 2][comp]
            edge[2 + comp, rows, :] = result[inner - 1][comp]
        return carry

    lax.fori_loop(0, LANES // 8, combine, 0)
    total = inner // 2 * LANES
    for comp in range(2):
        bins[comp, 0:8, :] = edge[2 + comp, LANES - 8 : LANES, :]
        bins[comp, 8 + total : 16 + total, :] = edge[comp, 0:8, :]
    for dest in range(groups):
        base = 8 + own * dest
        for comp in range(2):
            out_ref[dest, comp * own : (comp + 1) * own, :] = bins[comp, base : base + own, :]
            at = 2 * own + 4 * comp
            out_ref[dest, at : at + 2, :] = bins[comp, base - 2 : base, :]
            out_ref[dest, at + 2 : at + 4, :] = bins[comp, base + own : base + own + 2, :]


def local_transform(moved, groups, unit, w1, w2, t1, t2):
    inner = (moved.shape[1] - 8) * groups // LANES
    total = inner // 2 * LANES
    own = total // groups
    return pl.pallas_call(
        lambda *refs: local_kernel(groups, unit, *refs),
        out_shape=(
            jax.ShapeDtypeStruct((groups, 2 * own + 8, LANES), F32),
            jax.ShapeDtypeStruct((8, LANES), F32),
        ),
        in_specs=[VMEM_SPEC] * 5,
        out_specs=(VMEM_SPEC, VMEM_SPEC),
        compiler_params=ROOM,
        scratch_shapes=[
            pltpu.VMEM((inner // 2, 3 * LANES, 2 * LANES), BF16),
            pltpu.VMEM((inner // 2, 2 * LANES, 6 * LANES), BF16),
            pltpu.VMEM((inner, 2 * LANES, LANES), F32),
            pltpu.VMEM((2, total + 16, LANES), F32),
            pltpu.VMEM((4, LANES, LANES), F32),
        ],
    )(moved, w1, w2, t1, t2)


def matrix_kernel(taps_ref, stored_ref, out_ref, sent):
    row = lax.broadcasted_iota(jnp.int32, (LANES, LANES), 0)
    col = lax.broadcasted_iota(jnp.int32, (LANES, LANES), 1)
    below = col <= row

    def build(index, carry):
        lane = lax.broadcasted_iota(jnp.int32, (8, LANES), 1)
        source = (LANES - lane) & (LANES - 1)
        blocks = []
        for comp in range(2):
            taps = jnp.broadcast_to(taps_ref[index, pl.ds(comp, 1), :].astype(F32), (8, LANES))
            start = jnp.take_along_axis(taps, source, axis=1)
            start = jnp.broadcast_to(start[0:1, :], (LANES, LANES))
            ring = pltpu.roll(start, 0, 1, stride=1, stride_axis=0)
            blocks.append((jnp.where(below, ring, 0.0), jnp.where(below, 0.0, ring)))
        for part in range(2):
            real, imag = blocks[0][part], blocks[1][part]
            top = slice(part * LANES, (part + 1) * LANES)
            bottom = slice((2 + part) * LANES, (3 + part) * LANES)
            out_ref[index, top, 0:LANES] = real.astype(BF16)
            out_ref[index, top, LANES:] = imag.astype(BF16)
            out_ref[index, bottom, 0:LANES] = (-imag).astype(BF16)
            out_ref[index, bottom, LANES:] = real.astype(BF16)
        return carry

    lax.fori_loop(0, taps_ref.shape[0], build, 0)
    copies = [
        pltpu.make_async_copy(out_ref.at[index], stored_ref.at[index], sent.at[index])
        for index in range(out_ref.shape[0])
    ]
    for copy in copies:
        copy.start()
    for copy in copies:
        copy.wait()


def template_matrices(templates):
    count = templates.shape[0]
    return pl.pallas_call(
        matrix_kernel,
        out_shape=jax.ShapeDtypeStruct((4 * count, 4 * LANES, 2 * LANES), BF16),
        in_specs=[VMEM_SPEC],
        out_specs=pl.BlockSpec(memory_space=pl.ANY),
        scratch_shapes=[
            pltpu.VMEM((count, 4 * LANES, 2 * LANES), BF16),
            pltpu.SemaphoreType.DMA((count,)),
        ],
        compiler_params=WIDE,
        cost_estimate=pl.CostEstimate(
            flops=count * 40 * LANES * LANES,
            bytes_accessed=count * 24 * LANES * LANES,
            transcendentals=0,
        ),
    )(templates)


def power_kernel(
    place_ref,
    drift_ref,
    z_ref,
    level_ref,
    table_ref,
    matrices_ref,
    out_ref,
    bins,
    rim_rows,
    lhs,
    near,
    far,
    w_ref,
    arrived,
):
    count = w_ref.shape[0]

    def fetch(index):
        return pltpu.make_async_copy(matrices_ref.at[index], w_ref.at[index], arrived.at[index])

    for index in range(count):
        fetch(index).start()
    groups = z_ref.shape[0]
    own = z_ref.shape[1] // 2 - 4
    half = groups // 2
    main = groups * own
    scale = level_ref[...]

    def combine(chunk, carry):
        rows = pl.ds(pl.multiple_of(chunk * 8, 8), 8)
        rows_im = pl.ds(pl.multiple_of(own + chunk * 8, 8), 8)
        at = pl.ds(pl.multiple_of(8 + chunk * 8, 8), 8)
        powers = powered((table_ref[0, at, :], table_ref[1, at, :]), groups)
        values = [(z_ref[0, rows, :], z_ref[0, rows_im, :])]
        for step in range(1, groups):
            values.append(times((z_ref[step, rows, :], z_ref[step, rows_im, :]), powers[step]))
        result = small_fft(values)
        for step in range(groups):
            sign = level_ref[...] if step < half else -level_ref[...]
            bins[step, 0, at, :] = result[step][0] * level_ref[...]
            bins[step, 1, at, :] = result[step][1] * sign
        return carry

    lax.fori_loop(0, own // 8, combine, 0)
    rim = []
    for comp in range(2):
        rim.append(
            jnp.concatenate(
                [
                    table_ref[comp, 6:8, :],
                    table_ref[comp, 8 + own : 10 + own, :],
                    table_ref[comp, 6:8, :],
                    table_ref[comp, 8 + own : 10 + own, :],
                ]
            )
        )
    powers = powered((rim[0], rim[1]), groups)
    values = []
    for step in range(groups):
        both = z_ref[step, 2 * own : 2 * own + 8, :]
        value = (both, pltpu.roll(both, 4, 0))
        values.append(times(value, powers[step]) if step else value)
    result = small_fft(values)
    for step in range(groups):
        sign = scale if step < half else -scale
        for comp in range(2):
            value = result[step][comp] * (sign if comp else scale)
            bins[step, comp, 6:8, :] = value[0:2, :]
            bins[step, comp, 8 + own : 10 + own, :] = value[2:4, :]

    lane = lax.broadcasted_iota(jnp.int32, (8, LANES), 1)
    source = (LANES - lane) & (LANES - 1)
    rank = lax.broadcasted_iota(jnp.int32, (8, LANES), 0)
    for step in range(half, groups):
        for comp in range(2):
            for chunk in range(own // 8 + 1):
                here = bins[step, comp, 8 * chunk : 8 * chunk + 8, :]
                after = bins[step, comp, 8 * chunk + 1 : 8 * chunk + 9, :]
                value = jnp.where(lane == 0, after, jnp.take_along_axis(here, source, axis=1))
                if step == half and chunk == 0:
                    value = jnp.where(place_ref[0] == 0, 0.0, value)
                bins[step, comp, 8 * chunk : 8 * chunk + 8, :] = value
    for step in range(groups):
        for comp in range(2):
            for shift in range(2):
                at = 8 + shift if step < half else 8 - shift
                cols = slice((2 * comp + shift) * LANES, (2 * comp + shift + 1) * LANES)
                lhs[step * own : (step + 1) * own, cols] = bins[
                    step, comp, at : at + own, :
                ].astype(BF16)
                at = 8 + own + shift if step < half else 7 - shift
                rim_rows[2 * comp + shift, step : step + 1, :] = bins[step, comp, at : at + 1, :]
    for part in range(4):
        lhs[main:, part * LANES : (part + 1) * LANES] = rim_rows[part].astype(BF16)

    near[...] = jnp.zeros_like(near)
    far[...] = jnp.zeros_like(far)
    pieces = max(1, main // 512)
    edges = [main // pieces * piece for piece in range(pieces)] + [main + groups]

    batch = math.gcd(count, 8)

    def template(turn, carry):
        for member in range(batch):
            fetch(turn * batch + member).wait()
        for piece in range(pieces):
            rows = slice(edges[piece], edges[piece + 1])
            here, past = None, None
            for member in range(batch):
                index = turn * batch + member
                shift = drift_ref[index]
                response = jnp.dot(lhs[rows, :], w_ref[index], preferred_element_type=F32)
                power = response[:, :LANES] * response[:, :LANES]
                power = power + response[:, LANES:] * response[:, LANES:]
                rolled = pltpu.roll(power, (LANES - shift) & (LANES - 1), 1)
                inside = lax.broadcasted_iota(jnp.int32, rolled.shape, 1) < LANES - shift
                kept, moved = jnp.where(inside, rolled, 0.0), jnp.where(inside, 0.0, rolled)
                here = kept if here is None else here + kept
                past = moved if past is None else past + moved
            near[rows, :] += here
            far[rows, :] += past
        return carry

    lax.fori_loop(0, count // batch, template, 0)
    peak = jnp.zeros((8, LANES), F32)
    for step in range(groups):
        base = step * own
        spare = far[main + step : main + step + 1, :]
        if step < half:
            dest = 2 * step
            out_ref[dest, 0:own, :] = near[base : base + own, :] + far[base + 1 : base + own + 1, :]
            out_ref[dest, own - 1 : own, :] = near[base + own - 1 : base + own, :] + spare
        else:
            dest = 2 * (groups - 1 - step) + 1
            out_ref[dest, 0:own, :] = near[base : base + own, :] + far[base - 1 : base + own - 1, :]
            out_ref[dest, 0:1, :] = near[base : base + 1, :] + spare
        for chunk in range(own // 8):
            peak = jnp.maximum(peak, out_ref[dest, 8 * chunk : 8 * chunk + 8, :])
    scale, code = grow(jnp.max(peak), REACH)
    for dest in range(groups):
        out_ref[dest, 0:own, :] = out_ref[dest, 0:own, :] * scale
        out_ref[dest, own : own + 8, :] = jnp.full((8, LANES), code, F32)


def template_powers(place, drift, moved, level, table, matrices):
    groups = moved.shape[0]
    own = moved.shape[1] // 2 - 4
    rows = groups * own + groups
    return pl.pallas_call(
        power_kernel,
        out_shape=jax.ShapeDtypeStruct((groups, own + 8, LANES), F32),
        in_specs=[SMEM_SPEC, SMEM_SPEC] + [VMEM_SPEC] * 3 + [pl.BlockSpec(memory_space=pl.ANY)],
        out_specs=VMEM_SPEC,
        compiler_params=WIDE,
        scratch_shapes=[
            pltpu.VMEM((groups, 2, own + 24, LANES), F32),
            pltpu.VMEM((4, groups, LANES), F32),
            pltpu.VMEM((rows, 4 * LANES), BF16),
            pltpu.VMEM((rows, LANES), F32),
            pltpu.VMEM((rows, LANES), F32),
            pltpu.VMEM((drift.shape[0], 4 * LANES, 2 * LANES), BF16),
            pltpu.SemaphoreType.DMA((drift.shape[0],)),
        ],
    )(place, drift, moved, level, table, matrices)


def place_kernel(place_ref, power_ref, out_ref):
    groups, own = power_ref.shape[0], power_ref.shape[1] - 8
    total = groups * own
    flip = 7 - lax.broadcasted_iota(jnp.int32, (8, LANES), 0)

    @pl.when(place_ref[0] % 2 == 0)
    def _():
        for source in range(groups):
            factor = shrink(power_ref[source, own:, :], 1.0 / REACH)
            for chunk in range(own // 8):
                at = source * own + 8 * chunk
                value = power_ref[source, 8 * chunk : 8 * chunk + 8, :] * factor
                out_ref[at : at + 8, :] = value

    @pl.when(place_ref[0] % 2 == 1)
    def _():
        for source in range(groups):
            factor = shrink(power_ref[source, own:, :], 1.0 / REACH)
            for chunk in range(own // 8):
                at = total - source * own - 8 * chunk - 8
                value = power_ref[source, 8 * chunk : 8 * chunk + 8, :] * factor
                out_ref[at : at + 8, :] = jnp.take_along_axis(value, flip, axis=0)


def place_powers(place, moved):
    groups, own = moved.shape[0], moved.shape[1] - 8
    return pl.pallas_call(
        place_kernel,
        out_shape=jax.ShapeDtypeStruct((groups * own, LANES), F32),
        in_specs=[SMEM_SPEC, VMEM_SPEC],
        out_specs=VMEM_SPEC,
        compiler_params=ROOM,
    )(place, moved)


def exchange(value):
    moved = lax.all_to_all(value.astype(F16), AXES, split_axis=0, concat_axis=0, tiled=True)
    return moved.astype(F32)


def body(series, templates, drift):
    groups = lax.axis_size(AXES)
    place = lax.axis_index(AXES)
    samples = series.shape[0] * series.shape[1]
    length = samples * groups
    inner = samples // (LANES * LANES)
    total = inner // 2 * LANES
    own = total // groups
    index = np.arange(LANES, dtype=np.int64)
    w1 = jnp.asarray(first_matrix())
    w2 = jnp.asarray(second_matrix(2.0 / samples))
    t1 = jnp.asarray(table_pair(index[:, None] * index[None, :], LANES * LANES))
    t2 = jnp.asarray(table_pair(LANES * index[:, None] + index[None, :], samples))
    rows = np.arange(-8, total + 8, dtype=np.int64)
    wide = jnp.asarray(table_pair(LANES * rows[:, None] + index[None, :], length))
    table = lax.dynamic_slice_in_dim(wide, place * own, own + 16, axis=1)
    place = place.astype(jnp.int32).reshape(1)

    matrices = template_matrices(templates)
    moved = exchange(spread_samples(series, groups))
    unit = samples / 2 / math.sqrt(length)
    partial, level = local_transform(moved, groups, unit, w1, w2, t1, t2)
    moved = exchange(partial)
    power = template_powers(place, drift, moved, level, table, matrices)
    return place_powers(place, exchange(power))


def solution(mesh):
    in_specs = (P(("band", "gx", "gy"), None), P(), P())
    out_specs = P(("band", "gx", "gy"), None)
    return jax.shard_map(body, mesh=mesh, in_specs=in_specs, out_specs=out_specs, check_vma=False)
```

```python
import math

import jax
import jax.numpy as jnp
import numpy as np
from jax import lax
from jax.experimental import pallas as pl
from jax.experimental.pallas import tpu as pltpu
from jax.sharding import PartitionSpec as P

LANES = 128
AXES = ("gx", "gy")
VMEM_SPEC = pl.BlockSpec(memory_space=pltpu.VMEM)
SMEM_SPEC = pl.BlockSpec(memory_space=pltpu.SMEM)
F32 = jnp.float32
F16 = jnp.float16
STEPS = (64, 32, 16, 8, 4, 2, 1)
PEAK = 2.0**14
FLOOR = 1e-30
ROOM = pltpu.CompilerParams(vmem_limit_bytes=20 * 2**20)
WIDE = pltpu.CompilerParams(vmem_limit_bytes=50 * 2**20)
BF16 = jnp.bfloat16


def split_pair(table):
    high = np.asarray(table, np.float32).astype(BF16)
    low = (np.asarray(table, np.float64) - high.astype(np.float64)).astype(BF16)
    return high, low


def phases(product, length):
    angle = (product % length).astype(np.float64) * (-2.0 * np.pi / length)
    return np.cos(angle), np.sin(angle)


def first_matrix():
    index = np.arange(LANES, dtype=np.int64)
    real, imag = phases(index[:, None] * index[None, :], LANES)
    high, low = split_pair(np.concatenate([real, imag], axis=0))
    return np.concatenate([high, high, low], axis=1)


def second_matrix(gain):
    index = np.arange(LANES, dtype=np.int64)
    real, imag = phases(index[:, None] * index[None, :], LANES)
    real, imag = real * gain, imag * gain
    top = np.concatenate([real, -imag], axis=1)
    bottom = np.concatenate([imag, real], axis=1)
    high, low = split_pair(np.concatenate([top, bottom], axis=0))
    return np.concatenate([high, high, low], axis=1)


def table_pair(product, length):
    return np.stack(phases(product, length)).astype(np.float32)


def times(left, right):
    return (
        left[0] * right[0] - left[1] * right[1],
        left[0] * right[1] + left[1] * right[0],
    )


def small_fft(values):
    count = len(values)
    if count == 1:
        return values
    even = small_fft(values[0::2])
    odd = small_fft(values[1::2])
    head, tail = [], []
    for step in range(count // 2):
        real, imag = odd[step]
        if step == 0:
            turned = (real, imag)
        elif 4 * step == count:
            turned = (imag, -real)
        elif 8 * step == count:
            turned = ((real + imag) * math.sqrt(0.5), (imag - real) * math.sqrt(0.5))
        elif 8 * step == 3 * count:
            turned = ((imag - real) * math.sqrt(0.5), (real + imag) * -math.sqrt(0.5))
        else:
            angle = -2.0 * math.pi * step / count
            cosine, sine = math.cos(angle), math.sin(angle)
            turned = (real * cosine - imag * sine, real * sine + imag * cosine)
        head.append((even[step][0] + turned[0], even[step][1] + turned[1]))
        tail.append((even[step][0] - turned[0], even[step][1] - turned[1]))
    return head + tail


def powered(first, count):
    powers = [None, first]
    for step in range(2, count):
        half = step // 2
        powers.append(times(powers[half], powers[step - half]))
    return powers


def grow(peak, scale):
    code = 0.0
    for step in STEPS:
        grown = scale * 2.0**step
        fits = peak * grown <= PEAK
        scale = jnp.where(fits, grown, scale)
        code = jnp.where(fits, code + step, code)
    return scale, code


def shrink(code, scale):
    factor = jnp.full(code.shape, scale, F32)
    for step in STEPS:
        taken = code >= step
        factor = jnp.where(taken, factor * 2.0**-step, factor)
        code = jnp.where(taken, code - step, code)
    return factor


def columns_kernel(groups, series_ref, out_ref, turned):
    rows, width = series_ref.shape
    scale, code = grow(jnp.max(jnp.abs(series_ref[...])), 1.0)
    inner = out_ref.shape[1] - 8
    energy = jnp.sum(jnp.square(series_ref[...] * (scale / PEAK))) / (rows * width)
    rank = lax.broadcasted_iota(jnp.int32, (8, LANES), 0)
    notes = jnp.where(rank < 4, code, energy)
    for dest in range(groups):
        out_ref[dest, inner : inner + 8, :] = notes
    per_row = width // groups
    tall = rows // LANES
    for high in range(tall):
        turned[...] = (series_ref[high * LANES : (high + 1) * LANES, :] * scale).T
        for dest in range(groups):
            out_ref[dest, pl.ds(high, per_row, stride=tall), :] = turned[
                pl.ds(dest, per_row, stride=groups), :
            ]


def spread_samples(series, groups):
    rows, width = series.shape
    per_row = width // groups
    inner = rows * width // (LANES * LANES)
    tall = LANES // groups
    if per_row == inner:
        return pl.pallas_call(
            lambda *refs: columns_kernel(groups, *refs),
            out_shape=jax.ShapeDtypeStruct((groups, inner * tall + 8, LANES), F32),
            in_specs=[VMEM_SPEC],
            out_specs=VMEM_SPEC,
            compiler_params=ROOM,
            scratch_shapes=[pltpu.VMEM((width, LANES), F32)],
        )(series)
    scale, code = grow(jnp.max(jnp.abs(series)), F32(1.0))
    shaped = (series * scale).reshape(tall, LANES, inner // per_row, per_row, groups)
    moving = jnp.transpose(shaped, (4, 2, 3, 0, 1)).reshape(groups, inner * tall, LANES)
    energy = jnp.mean(jnp.square(series * (scale / PEAK)))
    notes = jnp.where(jnp.arange(8)[None, :, None] < 4, code, energy)
    return jnp.concatenate([moving, jnp.broadcast_to(notes, (groups, 8, LANES))], axis=1)


def local_kernel(
    groups,
    unit,
    y_ref,
    w1_ref,
    w2_ref,
    t1_ref,
    t2_ref,
    out_ref,
    level_ref,
    rhs,
    lhs,
    mid,
    bins,
    edge,
):
    inner = mid.shape[0]
    taken = y_ref.shape[1] - 8
    tall = taken // inner
    own = out_ref.shape[1] // 2 - 4
    codes = jnp.concatenate([y_ref[:, taken : taken + 4, :]] * 2, axis=1)
    energies = jnp.concatenate([y_ref[:, taken + 4 :, :]] * 2, axis=1)
    least = jnp.min(jnp.min(codes, axis=0), axis=0, keepdims=True)
    least = jnp.broadcast_to(least, (8, LANES))
    level_ref[0] = shrink(least, unit)
    factor = shrink(codes - least[None], 1.0)
    mean = jnp.sum(energies * (factor * factor), axis=0) * (1.0 / groups)
    level_ref[1] = jnp.sqrt(mean) * shrink(least, PEAK)
    factor = factor[:, :tall, :] if tall <= 8 else factor[:, :1, :]
    for pair in range(inner // 2):
        for part in range(2):
            step = 2 * pair + part
            block = y_ref[:, step * tall : (step + 1) * tall, :] * factor
            block = block.reshape(LANES, LANES)
            high = block.astype(BF16)
            low = (block - high.astype(F32)).astype(BF16)
            cols = slice(part * LANES, (part + 1) * LANES)
            rhs[pair, 0:LANES, cols] = high
            rhs[pair, LANES : 2 * LANES, cols] = low
            rhs[pair, 2 * LANES : 3 * LANES, cols] = high
    for pair in range(inner // 2):
        first = jnp.dot(w1_ref[...], rhs[pair], preferred_element_type=F32)
        for part in range(2):
            cols = slice(part * LANES, (part + 1) * LANES)
            turned = times(
                (first[:LANES, cols], first[LANES:, cols]), (t1_ref[0], t1_ref[1])
            )
            rows = slice(part * LANES, (part + 1) * LANES)
            for comp in range(2):
                high = turned[comp].astype(BF16)
                low = (turned[comp] - high.astype(F32)).astype(BF16)
                at = comp * LANES
                lhs[pair, rows, at : at + LANES] = high
                lhs[pair, rows, 2 * LANES + at : 3 * LANES + at] = low
                lhs[pair, rows, 4 * LANES + at : 5 * LANES + at] = high
    for pair in range(inner // 2):
        second = lax.dot_general(
            w2_ref[...], lhs[pair], (((1,), (1,)), ((), ())), preferred_element_type=F32
        )
        mid[2 * pair] = second[:, :LANES]
        mid[2 * pair + 1] = second[:, LANES:]

    def combine(chunk, carry):
        rows = pl.ds(pl.multiple_of(chunk * 8, 8), 8)
        rows_im = pl.ds(pl.multiple_of(LANES + chunk * 8, 8), 8)
        powers = powered((t2_ref[0, rows, :], t2_ref[1, rows, :]), inner)
        values = [(mid[0, rows, :], mid[0, rows_im, :])]
        for step in range(1, inner):
            values.append(times((mid[step, rows, :], mid[step, rows_im, :]), powers[step]))
        result = small_fft(values)
        for comp in range(2):
            for step in range(inner // 2):
                at = pl.multiple_of(8 + step * LANES + chunk * 8, 8)
                bins[comp, pl.ds(at, 8), :] = result[step][comp]
            edge[comp, rows, :] = result[inner // 2][comp]
            edge[2 + comp, rows, :] = result[inner - 1][comp]
        return carry

    lax.fori_loop(0, LANES // 8, combine, 0)
    total = inner // 2 * LANES
    for comp in range(2):
        bins[comp, 0:8, :] = edge[2 + comp, LANES - 8 : LANES, :]
        bins[comp, 8 + total : 16 + total, :] = edge[comp, 0:8, :]
    for dest in range(groups):
        base = 8 + own * dest
        for comp in range(2):
            out_ref[dest, comp * own : (comp + 1) * own, :] = bins[comp, base : base + own, :]
            at = 2 * own + 4 * comp
            out_ref[dest, at : at + 2, :] = bins[comp, base - 2 : base, :]
            out_ref[dest, at + 2 : at + 4, :] = bins[comp, base + own : base + own + 2, :]


def local_transform(moved, groups, unit, w1, w2, t1, t2):
    inner = (moved.shape[1] - 8) * groups // LANES
    total = inner // 2 * LANES
    own = total // groups
    return pl.pallas_call(
        lambda *refs: local_kernel(groups, unit, *refs),
        out_shape=(
            jax.ShapeDtypeStruct((groups, 2 * own + 8, LANES), F32),
            jax.ShapeDtypeStruct((2, 8, LANES), F32),
        ),
        in_specs=[VMEM_SPEC] * 5,
        out_specs=(VMEM_SPEC, VMEM_SPEC),
        compiler_params=ROOM,
        scratch_shapes=[
            pltpu.VMEM((inner // 2, 3 * LANES, 2 * LANES), BF16),
            pltpu.VMEM((inner // 2, 2 * LANES, 6 * LANES), BF16),
            pltpu.VMEM((inner, 2 * LANES, LANES), F32),
            pltpu.VMEM((2, total + 16, LANES), F32),
            pltpu.VMEM((4, LANES, LANES), F32),
        ],
    )(moved, w1, w2, t1, t2)


def matrix_kernel(taps_ref, stored_ref, out_ref, sent):
    row = lax.broadcasted_iota(jnp.int32, (LANES, LANES), 0)
    col = lax.broadcasted_iota(jnp.int32, (LANES, LANES), 1)
    below = col <= row

    def build(index, carry):
        lane = lax.broadcasted_iota(jnp.int32, (8, LANES), 1)
        source = (LANES - lane) & (LANES - 1)
        blocks = []
        for comp in range(2):
            taps = jnp.broadcast_to(taps_ref[index, pl.ds(comp, 1), :].astype(F32), (8, LANES))
            start = jnp.take_along_axis(taps, source, axis=1)
            start = jnp.broadcast_to(start[0:1, :], (LANES, LANES))
            ring = pltpu.roll(start, 0, 1, stride=1, stride_axis=0)
            blocks.append((jnp.where(below, ring, 0.0), jnp.where(below, 0.0, ring)))
        for part in range(2):
            real, imag = blocks[0][part], blocks[1][part]
            top = slice(part * LANES, (part + 1) * LANES)
            out_ref[index, top, 0:LANES] = real.astype(BF16)
            out_ref[index, top, LANES:] = imag.astype(BF16)
        return carry

    lax.fori_loop(0, taps_ref.shape[0], build, 0)
    copies = [
        pltpu.make_async_copy(out_ref.at[index], stored_ref.at[index], sent.at[index])
        for index in range(out_ref.shape[0])
    ]
    for copy in copies:
        copy.start()
    for copy in copies:
        copy.wait()


def template_matrices(templates):
    count = templates.shape[0]
    return pl.pallas_call(
        matrix_kernel,
        out_shape=jax.ShapeDtypeStruct((8 * count, 2 * LANES, 2 * LANES), BF16),
        in_specs=[VMEM_SPEC],
        out_specs=pl.BlockSpec(memory_space=pl.ANY),
        scratch_shapes=[
            pltpu.VMEM((count, 2 * LANES, 2 * LANES), BF16),
            pltpu.SemaphoreType.DMA((count,)),
        ],
        compiler_params=WIDE,
        cost_estimate=pl.CostEstimate(
            flops=count * 40 * LANES * LANES,
            bytes_accessed=count * 24 * LANES * LANES,
            transcendentals=0,
        ),
    )(templates)


def power_kernel(
    place_ref,
    drift_ref,
    z_ref,
    level_ref,
    step_ref,
    table_ref,
    matrices_ref,
    out_ref,
    bins,
    rim_rows,
    lhs,
    near,
    far,
    w_ref,
    arrived,
):
    count = w_ref.shape[0]

    def fetch(index):
        top = w_ref.at[index, pl.ds(0, 2 * LANES), :]
        return pltpu.make_async_copy(matrices_ref.at[index], top, arrived.at[index])

    for index in range(count):
        fetch(index).start()
    groups = z_ref.shape[0]
    own = z_ref.shape[1] // 2 - 4
    half = groups // 2
    main = groups * own
    scale = level_ref[...]

    def combine(chunk, carry):
        rows = pl.ds(pl.multiple_of(chunk * 8, 8), 8)
        rows_im = pl.ds(pl.multiple_of(own + chunk * 8, 8), 8)
        at = pl.ds(pl.multiple_of(8 + chunk * 8, 8), 8)
        powers = powered((table_ref[0, at, :], table_ref[1, at, :]), groups)
        values = [(z_ref[0, rows, :], z_ref[0, rows_im, :])]
        for step in range(1, groups):
            values.append(times((z_ref[step, rows, :], z_ref[step, rows_im, :]), powers[step]))
        result = small_fft(values)
        for step in range(groups):
            sign = level_ref[...] if step < half else -level_ref[...]
            bins[step, 0, at, :] = result[step][0] * level_ref[...]
            bins[step, 1, at, :] = result[step][1] * sign
        return carry

    lax.fori_loop(0, own // 8, combine, 0)
    rim = []
    for comp in range(2):
        rim.append(
            jnp.concatenate(
                [
                    table_ref[comp, 6:8, :],
                    table_ref[comp, 8 + own : 10 + own, :],
                    table_ref[comp, 6:8, :],
                    table_ref[comp, 8 + own : 10 + own, :],
                ]
            )
        )
    powers = powered((rim[0], rim[1]), groups)
    values = []
    for step in range(groups):
        both = z_ref[step, 2 * own : 2 * own + 8, :]
        value = (both, pltpu.roll(both, 4, 0))
        values.append(times(value, powers[step]) if step else value)
    result = small_fft(values)
    for step in range(groups):
        sign = scale if step < half else -scale
        for comp in range(2):
            value = result[step][comp] * (sign if comp else scale)
            bins[step, comp, 6:8, :] = value[0:2, :]
            bins[step, comp, 8 + own : 10 + own, :] = value[2:4, :]

    lane = lax.broadcasted_iota(jnp.int32, (8, LANES), 1)
    source = (LANES - lane) & (LANES - 1)
    rank = lax.broadcasted_iota(jnp.int32, (8, LANES), 0)
    for step in range(half, groups):
        for comp in range(2):
            for chunk in range(own // 8 + 1):
                here = bins[step, comp, 8 * chunk : 8 * chunk + 8, :]
                after = bins[step, comp, 8 * chunk + 1 : 8 * chunk + 9, :]
                value = jnp.where(lane == 0, after, jnp.take_along_axis(here, source, axis=1))
                if step == half and chunk == 0:
                    value = jnp.where(place_ref[0] == 0, 0.0, value)
                bins[step, comp, 8 * chunk : 8 * chunk + 8, :] = value
    for step in range(groups):
        for comp in range(2):
            for shift in range(2):
                at = 8 + shift if step < half else 8 - shift
                cols = slice((2 * comp + shift) * LANES, (2 * comp + shift + 1) * LANES)
                lhs[step * own : (step + 1) * own, cols] = bins[
                    step, comp, at : at + own, :
                ].astype(BF16)
                at = 8 + own + shift if step < half else 7 - shift
                rim_rows[2 * comp + shift, step : step + 1, :] = bins[step, comp, at : at + 1, :]
    for part in range(4):
        lhs[main:, part * LANES : (part + 1) * LANES] = rim_rows[part].astype(BF16)

    near[...] = jnp.zeros_like(near)
    far[...] = jnp.zeros_like(far)
    pieces = max(1, main // 512)
    edges = [main // pieces * piece for piece in range(pieces)] + [main + groups]

    batch = math.gcd(count, 8)

    def template(turn, carry):
        for member in range(batch):
            fetch(turn * batch + member).wait()
        for member in range(batch):
            index = turn * batch + member
            w_ref[index, 2 * LANES :, 0:LANES] = -w_ref[index, 0 : 2 * LANES, LANES:]
            w_ref[index, 2 * LANES :, LANES:] = w_ref[index, 0 : 2 * LANES, 0:LANES]
        for piece in range(pieces):
            rows = slice(edges[piece], edges[piece + 1])
            here, past = None, None
            for member in range(batch):
                index = turn * batch + member
                shift = drift_ref[index]
                response = jnp.dot(lhs[rows, :], w_ref[index], preferred_element_type=F32)
                power = response[:, :LANES] * response[:, :LANES]
                power = power + response[:, LANES:] * response[:, LANES:]
                rolled = pltpu.roll(power, (LANES - shift) & (LANES - 1), 1)
                inside = lax.broadcasted_iota(jnp.int32, rolled.shape, 1) < LANES - shift
                kept, moved = jnp.where(inside, rolled, 0.0), jnp.where(inside, 0.0, rolled)
                here = kept if here is None else here + kept
                past = moved if past is None else past + moved
            near[rows, :] += here
            far[rows, :] += past
        return carry

    lax.fori_loop(0, count // batch, template, 0)
    gain = jnp.broadcast_to((1.0 / step_ref[...])[0:1, :], (own, LANES))
    for step in range(groups):
        base = step * own
        spare = far[main + step : main + step + 1, :]
        if step < half:
            dest, edge = 2 * step, own - 1
            total = near[base : base + own, :] + far[base + 1 : base + own + 1, :]
        else:
            dest, edge = 2 * (groups - 1 - step) + 1, 0
            total = near[base : base + own, :] + far[base - 1 : base + own - 1, :]
        out_ref[dest, :, :] = jnp.sqrt(total) * gain
        last = near[base + edge : base + edge + 1, :] + spare
        out_ref[dest, edge : edge + 1, :] = jnp.sqrt(last) * gain[0:1, :]


def template_powers(place, drift, moved, level, step, table, matrices):
    groups = moved.shape[0]
    own = moved.shape[1] // 2 - 4
    rows = groups * own + groups
    return pl.pallas_call(
        power_kernel,
        out_shape=jax.ShapeDtypeStruct((groups, own, LANES), F32),
        in_specs=[SMEM_SPEC, SMEM_SPEC] + [VMEM_SPEC] * 4 + [pl.BlockSpec(memory_space=pl.ANY)],
        out_specs=VMEM_SPEC,
        compiler_params=WIDE,
        scratch_shapes=[
            pltpu.VMEM((groups, 2, own + 24, LANES), F32),
            pltpu.VMEM((4, groups, LANES), F32),
            pltpu.VMEM((rows, 4 * LANES), BF16),
            pltpu.VMEM((rows, LANES), F32),
            pltpu.VMEM((rows, LANES), F32),
            pltpu.VMEM((drift.shape[0], 4 * LANES, 2 * LANES), BF16),
            pltpu.SemaphoreType.DMA((drift.shape[0],)),
        ],
    )(place, drift, moved, level, step, table, matrices)


def place_kernel(place_ref, power_ref, step_ref, out_ref):
    groups, own = power_ref.shape[0], power_ref.shape[1]
    total = groups * own
    flip = 7 - lax.broadcasted_iota(jnp.int32, (8, LANES), 0)

    @pl.when(place_ref[0] % 2 == 0)
    def _():
        for source in range(groups):
            for chunk in range(own // 8):
                at = source * own + 8 * chunk
                value = jnp.square(power_ref[source, 8 * chunk : 8 * chunk + 8, :] * step_ref[...])
                out_ref[at : at + 8, :] = value

    @pl.when(place_ref[0] % 2 == 1)
    def _():
        for source in range(groups):
            for chunk in range(own // 8):
                at = total - source * own - 8 * chunk - 8
                value = jnp.square(power_ref[source, 8 * chunk : 8 * chunk + 8, :] * step_ref[...])
                out_ref[at : at + 8, :] = jnp.take_along_axis(value, flip, axis=0)


def place_powers(place, moved, step):
    groups, own = moved.shape[0], moved.shape[1]
    return pl.pallas_call(
        place_kernel,
        out_shape=jax.ShapeDtypeStruct((groups * own, LANES), F32),
        in_specs=[SMEM_SPEC, VMEM_SPEC, VMEM_SPEC],
        out_specs=VMEM_SPEC,
        compiler_params=ROOM,
    )(place, moved, step)


def exchange(value):
    moved = lax.all_to_all(value.astype(F16), AXES, split_axis=0, concat_axis=0, tiled=True)
    return moved.astype(F32)


def body(series, templates, drift):
    groups = lax.axis_size(AXES)
    place = lax.axis_index(AXES)
    samples = series.shape[0] * series.shape[1]
    length = samples * groups
    inner = samples // (LANES * LANES)
    total = inner // 2 * LANES
    own = total // groups
    index = np.arange(LANES, dtype=np.int64)
    w1 = jnp.asarray(first_matrix())
    w2 = jnp.asarray(second_matrix(2.0 / samples))
    t1 = jnp.asarray(table_pair(index[:, None] * index[None, :], LANES * LANES))
    t2 = jnp.asarray(table_pair(LANES * index[:, None] + index[None, :], samples))
    rows = np.arange(-8, total + 8, dtype=np.int64)
    wide = jnp.asarray(table_pair(LANES * rows[:, None] + index[None, :], length))
    table = lax.dynamic_slice_in_dim(wide, place * own, own + 16, axis=1)
    place = place.astype(jnp.int32).reshape(1)

    matrices = template_matrices(templates)
    moved = exchange(spread_samples(series, groups))
    unit = samples / 2 / math.sqrt(length)
    partial, level = local_transform(moved, groups, unit, w1, w2, t1, t2)
    moved = exchange(partial)
    taps = 2 * templates.shape[0] * templates.shape[2] ** 2
    bound = math.sqrt(taps * length) * jnp.max(jnp.abs(templates.astype(F32))) * level[1]
    step = jnp.maximum(bound, FLOOR) * 2.0**-15
    power = template_powers(place, drift, moved, level[0], step, table, matrices)
    return place_powers(place, exchange(power), step)


def solution(mesh):
    in_specs = (P(("band", "gx", "gy"), None), P(), P())
    out_specs = P(("band", "gx", "gy"), None)
    return jax.shard_map(body, mesh=mesh, in_specs=in_specs, out_specs=out_specs, check_vma=False)
```
